256 devices in a mesh: pix: 16 (over y_lo, x, core), ion: 16 (over y_hi, z).
Axes of the slice: x: 4, y: 4 (y_hi: 2, y_lo: 2; y = y_hi * 2 + y_lo), z: 8, core: 2. Of those that a mesh axis runs over, the one named last changes fastest.
Arguments:
- images: bfloat16 [20480, 32768], P('ion', 'pix')
- stencil: float32 [5, 32768], P(None, 'pix'), may hold values from 0.05 to 0.4
- pairs: int32 [768, 2], P('ion'), may hold values from 0 to 159, as said below
- live: int32 [16], P('ion'), may hold values from 16 to 48, as said below
- rule_of_block: int32 [160], replicated, may hold values from 0 to 63
- adduct: bfloat16 [64, 128, 128], P('ion'), may hold values from -6 to 6
Outputs:
- smoothed: bfloat16 [20480, 32768], P('ion', 'pix')
- scores: bfloat16 [768, 128, 128], P('ion', 'pix')
The draws below stay inside these ranges and needn't reach their ends.
Inputs may be any that keep to these rules, and one draw needn't show every extreme that they name: Slot s belongs to ion block range of index s // 48 of ion: a lies in that index's own 20480 // (128 * 16) blocks, and |a - b| <= 3. Entries of unused slots are valid pairs too. `live`: some index of ion uses all its slots.
All inputs are finite; a program needn't handle non-finite values.
Results may differ from the reference program's by a relative error of at most 0.0053.
Values may be sent and summed in bfloat16 or wider, within the bound.
A program may use at most 192 MiB of HBM per device.

```python
import math
import jax
import jax.numpy as jnp
from jax import lax

IONS = 20480
BLOCK = 128
RULES = 64
REACH = 3
PAIRS_DEV = 48
PIXELS = 32768
NBLK = 160
PAIR_SLOTS = 768
N_ION = 16


def draw_images(key, part):
    key_row_block, key_cols, key_base = jax.random.split(key, 3)
    row_scale = jnp.exp(jax.random.uniform(key_row_block, (IONS, 1), jnp.float32, math.log(0.3), math.log(3.0)))
    position = jnp.arange(PIXELS, dtype=jnp.float32) / max(PIXELS - 1, 1)
    col_scale = jnp.exp(jax.random.uniform(key_cols, (1, PIXELS), jnp.float32, math.log(0.3), math.log(3.0)))
    col_scale = col_scale * (0.5 + position)[None, :]
    base = jax.random.normal(key_base, (IONS, PIXELS), jnp.float32)
    return (base * row_scale * col_scale).astype(jnp.bfloat16)


def pair_tables(key):
    base = jax.random.fold_in(key, 7717)
    key_live, key_top, key_block, key_offset = jax.random.split(base, 4)
    local_blocks = IONS // (BLOCK * N_ION)
    live_counts = jax.random.randint(key_live, (N_ION,), PAIRS_DEV // 3, PAIRS_DEV + 1)
    top_index = jax.random.randint(key_top, (), 0, N_ION)
    live_counts = live_counts.at[top_index].set(PAIRS_DEV)
    block_local = jax.random.randint(key_block, (N_ION, PAIRS_DEV), 0, local_blocks)
    offsets = jax.random.randint(key_offset, (N_ION, PAIRS_DEV), -REACH, REACH + 1)
    block_local = block_local.at[:, 0].set(0).at[:, 1].set(local_blocks - 1)
    offsets = offsets.at[:, 0].set(-REACH).at[:, 1].set(REACH)
    device_ids = jnp.arange(N_ION, dtype=jnp.int32)[:, None]
    first_block = device_ids * local_blocks + block_local
    partner_block = jnp.clip(first_block + offsets, 0, NBLK - 1)
    table = jnp.stack([first_block, partner_block], axis=-1).reshape(PAIR_SLOTS, 2)
    return (table.astype(jnp.int32), live_counts.astype(jnp.int32))


def draw_pairs(key, part):
    return pair_tables(key)[0]


def draw_live(key, part):
    return pair_tables(key)[1]


def plant(values, own_key, low, high):
    dims = values.shape
    spot = [jax.random.randint(jax.random.fold_in(own_key, axis), (), 0, dims[axis]) for axis in range(len(dims))]
    values = values.at[tuple(spot)].set(low)
    longest = dims.index(max(dims))
    spot[longest] = (spot[longest] + 1) % dims[longest]
    return values.at[tuple(spot)].set(high)


def steps_of(key, shape, cuts, smallest, top_value):
    level = 1.0
    for axis_at, shards_of in cuts:
        heights = jax.random.uniform(jax.random.fold_in(jax.random.fold_in(key, 6), axis_at), (shards_of,), jnp.float32, smallest / len(cuts), top_value / len(cuts))
        level = level * jnp.repeat(jnp.exp(heights), shape[axis_at] // shards_of).reshape((-1,) + (1,) * (len(shape) - 1 - axis_at))
    return level


def noise(rng, dims, width, bound, cuts=(), held_as=jnp.bfloat16):
    entries = jax.random.normal(rng, dims, jnp.float32) * width
    if len(cuts) > 0:
        entries = steps_of(rng, dims, cuts, -0.22, 0.18) * entries
    return jnp.clip(entries, min=-bound, max=bound).astype(held_as)


def setup_inputs(seed: int = 0) -> dict:
    arg_keys = jax.random.split(jax.random.key(seed), 7)
    images = draw_images(jax.random.fold_in(arg_keys[6], 71), 0)
    stencil = jnp.clip(0.05 + 0.35 * jax.random.uniform(arg_keys[1], (5, PIXELS), jnp.float32) ** steps_of(arg_keys[1], (5, PIXELS), ((1, 16),), -0.2, 0.2), 0.05, 0.4)
    pairs = draw_pairs(jax.random.fold_in(arg_keys[6], 71), 0)
    live = draw_live(jax.random.fold_in(arg_keys[6], 71), 0)
    rule_of_block = plant(jax.random.randint(arg_keys[4], (NBLK,), 0, RULES), jax.random.fold_in(arg_keys[4], 1), 0, RULES - 1).astype(jnp.int32)
    adduct = noise(arg_keys[5], (RULES, BLOCK, BLOCK), 1.0, 6.0, ((0, 16),))
    return dict(images=images, stencil=stencil, pairs=pairs, live=live, rule_of_block=rule_of_block, adduct=adduct)


def smooth_block(pieces):
    rows, weights = pieces
    padded = jnp.pad(rows.astype(jnp.float32), ((0, 0), (2, 2)))
    total = jnp.zeros(rows.shape, jnp.float32)
    for tap in range(5):
        total = total + weights[tap][None, :] * padded[:, tap:tap + PIXELS]
    return total.astype(jnp.bfloat16)

def reference(images, stencil, pairs, live, rule_of_block, adduct):
    blocks = images.reshape(NBLK, BLOCK, PIXELS)

    def one_block(rows):
        return smooth_block((rows, stencil))
    smoothed = lax.map(one_block, blocks).reshape(IONS, PIXELS)

    def block_energy(rows):
        values = rows.astype(jnp.float32)
        return lax.optimization_barrier(jnp.mean(values * values, axis=1))
    energy = lax.map(block_energy, smoothed.reshape(NBLK, BLOCK, PIXELS)).reshape(IONS)
    inverse = 1.0 / jnp.sqrt(energy + 1e-06)

    def one_pair(pair):
        first = (pair[0] * BLOCK).astype(jnp.int32)
        second = (pair[1] * BLOCK).astype(jnp.int32)
        left_operand = lax.dynamic_slice_in_dim(smoothed, first, BLOCK, 0)
        right_operand = lax.dynamic_slice_in_dim(smoothed, second, BLOCK, 0)
        gram = jnp.dot(left_operand, right_operand.T, preferred_element_type=jnp.float32)
        inv_left = lax.dynamic_slice_in_dim(inverse, first, BLOCK, 0)
        inv_right = lax.dynamic_slice_in_dim(inverse, second, BLOCK, 0)
        coloc = (gram * inv_left[:, None] * inv_right[None, :] / PIXELS).astype(jnp.bfloat16)
        table = adduct[rule_of_block[pair[1]]]
        return jnp.dot(coloc, table, preferred_element_type=jnp.float32)
    scores = lax.map(one_pair, pairs)
    slot_numbers = jnp.arange(PAIR_SLOTS, dtype=jnp.int32)
    used = slot_numbers % PAIRS_DEV < live[slot_numbers // PAIRS_DEV]
    scores = jnp.where(used[:, None, None], scores, 0.0).astype(jnp.bfloat16)
    return (smoothed, scores)
```

```python
import jax
import jax.numpy as jnp
from jax import lax
from jax.experimental import pallas as pl
from jax.experimental.pallas import tpu as pltpu
from jax.sharding import PartitionSpec as P

REACH = 3


def extended_2(array, sides, width):
    for axis, dim in sides:
        size, length = (lax.axis_size(axis), array.shape[dim])
        up = [(i, (i + 1) % size) for i in range(size - 1)]
        down = [(j, i) for i, j in up]
        last = lax.slice_in_dim(array, length - width, length, axis=dim)
        first = lax.slice_in_dim(array, 0, width, axis=dim)
        before = lax.ppermute(last, axis, up)
        after = lax.ppermute(first, axis, down)
        array = jnp.concatenate([before, array, after], axis=dim)
    return array


def gram_kernel(shares, rel_ref, ext_ref, out_ref):
    block = out_ref.shape[3]
    slots = out_ref.shape[1]
    rows = out_ref.shape[2]

    def body(s, carry):
        ra = rel_ref[2 * s]
        rb = rel_ref[2 * s + 1]
        left = ext_ref[pl.ds(pl.multiple_of(ra * block, block), block), :]
        right = ext_ref[pl.ds(pl.multiple_of(rb * block, block), block), :]
        g = lax.dot_general(
            left, right, (((1,), (1,)), ((), ())), preferred_element_type=jnp.float32
        )
        for q in range(shares):
            out_ref[q, s] = g[q * rows : (q + 1) * rows, :]
        return carry

    lax.fori_loop(0, slots, body, 0)


def pair_grams(relative, extended, shares, block):
    slots = relative.shape[0]
    rows = block // shares
    pix_local = extended.shape[1]
    flat = relative.reshape(-1).astype(jnp.int32)
    return pl.pallas_call(
        lambda *refs: gram_kernel(shares, *refs),
        out_shape=jax.ShapeDtypeStruct((shares, slots, rows, block), jnp.float32),
        in_specs=[
            pl.BlockSpec(memory_space=pltpu.SMEM),
            pl.BlockSpec(memory_space=pltpu.VMEM),
        ],
        out_specs=pl.BlockSpec(memory_space=pltpu.VMEM),
        compiler_params=pltpu.CompilerParams(vmem_limit_bytes=48 * 1024 * 1024),
        cost_estimate=pl.CostEstimate(
            flops=2 * slots * block * block * pix_local,
            transcendentals=0,
            bytes_accessed=extended.size * 2 + slots * block * block * 4,
        ),
    )(flat, extended)


def on_device(images, stencil, pairs, live, rule_of_block, adduct):
    local_rows, pix_local = images.shape
    block = adduct.shape[1]
    local_blocks = local_rows // block
    shares = lax.axis_size("pix")
    rows = block // shares
    padded = extended_2(images, (("pix", 1),), 2)
    total = jnp.zeros((local_rows, pix_local), jnp.float32)
    for tap in range(5):
        total = total + stencil[tap][None, :] * padded[:, tap : tap + pix_local].astype(jnp.float32)
    smoothed = total.astype(jnp.bfloat16)
    extended = extended_2(smoothed, (("ion", 0),), REACH * block)
    values = extended.astype(jnp.float32)
    squares = jnp.sum(values * values, axis=1)
    pixel_count = pix_local * shares
    energy = lax.psum(squares, "pix") / pixel_count
    inverse = 1.0 / jnp.sqrt(energy + 1e-06)
    lookup_tables = lax.all_gather(adduct, "ion", axis=0, tiled=True)
    first = lax.axis_index("ion") * local_blocks
    inv_blocks = inverse.reshape(local_blocks + 2 * REACH, block)
    slots = pairs.shape[0]
    relative = pairs - first + REACH

    grams = pair_grams(relative, extended, shares, block)
    gram = lax.psum_scatter(grams, "pix", scatter_dimension=0, tiled=True)[0]

    offset = lax.axis_index("pix") * rows
    inv_left = lax.dynamic_slice_in_dim(
        jnp.take(inv_blocks, relative[:, 0], axis=0), offset, rows, 1
    )
    inv_right = jnp.take(inv_blocks, relative[:, 1], axis=0)
    rules = jnp.take(rule_of_block, pairs[:, 1], axis=0)
    matrices = jnp.take(lookup_tables, rules, axis=0)
    coloc = (gram * inv_left[:, :, None] * inv_right[:, None, :] / pixel_count).astype(jnp.bfloat16)
    scores = jnp.einsum("src,scd->srd", coloc, matrices, preferred_element_type=jnp.float32)
    used = jnp.arange(slots, dtype=jnp.int32) < live[0]
    scores = jnp.where(used[:, None, None], scores, 0.0).astype(jnp.bfloat16)
    return (smoothed, scores)


def solution(mesh):
    return jax.shard_map(
        on_device,
        mesh=mesh,
        in_specs=(
            P("ion", "pix"),
            P(None, "pix"),
            P("ion", None),
            P("ion"),
            P(),
            P("ion", None, None),
        ),
        out_specs=(P("ion", "pix"), P("ion", "pix", None)),
        check_vma=False,
    )
```

```python
import jax
import jax.numpy as jnp
from jax import lax
from jax.experimental import pallas as pl
from jax.experimental.pallas import tpu as pltpu
from jax.sharding import PartitionSpec as P

REACH = 3


def extended_2(array, sides, width):
    for axis, dim in sides:
        size, length = (lax.axis_size(axis), array.shape[dim])
        up = [(i, (i + 1) % size) for i in range(size - 1)]
        down = [(j, i) for i, j in up]
        last = lax.slice_in_dim(array, length - width, length, axis=dim)
        first = lax.slice_in_dim(array, 0, width, axis=dim)
        before = lax.ppermute(last, axis, up)
        after = lax.ppermute(first, axis, down)
        array = jnp.concatenate([before, array, after], axis=dim)
    return array


def gram_kernel(shares, rel_ref, ext_ref, out_ref):
    block = out_ref.shape[-1]
    slots = out_ref.shape[-3]
    rows = out_ref.shape[-2]

    def body(s, carry):
        ra = rel_ref[2 * s]
        rb = rel_ref[2 * s + 1]
        left = ext_ref[pl.ds(pl.multiple_of(ra * block, block), block), :]
        right = ext_ref[pl.ds(pl.multiple_of(rb * block, block), block), :]
        g = lax.dot_general(
            left, right, (((1,), (1,)), ((), ())), preferred_element_type=jnp.float32
        )
        for q in range(shares):
            out_ref[q % 2, (q // 2) % 4, q // 8, s] = g[q * rows : (q + 1) * rows, :]
        return carry

    lax.fori_loop(0, slots, body, 0)


def pair_grams(relative, extended, shares, block):
    slots = relative.shape[0]
    rows = block // shares
    pix_local = extended.shape[1]
    flat = relative.reshape(-1).astype(jnp.int32)
    return pl.pallas_call(
        lambda *refs: gram_kernel(shares, *refs),
        out_shape=jax.ShapeDtypeStruct((2, 4, 2, slots, rows, block), jnp.float32),
        in_specs=[
            pl.BlockSpec(memory_space=pltpu.SMEM),
            pl.BlockSpec(memory_space=pltpu.VMEM),
        ],
        out_specs=pl.BlockSpec(memory_space=pltpu.VMEM),
        compiler_params=pltpu.CompilerParams(vmem_limit_bytes=48 * 1024 * 1024),
        cost_estimate=pl.CostEstimate(
            flops=2 * slots * block * block * pix_local,
            transcendentals=0,
            bytes_accessed=extended.size * 2 + slots * block * block * 4,
        ),
    )(flat, extended)


MESH = pl.DeviceIdType.MESH


def scatter_kernel(g_ref, e_ref, out_ref, eout_ref, r1, s1, recv_r, recv_l, acc_r, acc_l, tbuf, r3, ebuf, send_sem, recv_sem):
    p = lax.axis_index("pix")
    c = p % 2
    x = (p // 2) % 4
    yl = p // 8
    partner = p + 1 - 2 * c
    right = (yl * 4 + (x + 1) % 4) * 2 + c
    left = (yl * 4 + (x + 3) % 4) * 2 + c
    ypart = ((1 - yl) * 4 + x) * 2 + c

    barrier = pltpu.get_barrier_semaphore()
    for peer in (partner, right, left, ypart):
        pl.semaphore_signal(barrier, 1, device_id={"pix": peer}, device_id_type=MESH)
    pl.semaphore_wait(barrier, 4)

    def remote(src, dst, k, peer):
        return pltpu.make_async_remote_copy(
            src_ref=src, dst_ref=dst, send_sem=send_sem.at[k], recv_sem=recv_sem.at[k],
            device_id={"pix": peer}, device_id_type=MESH,
        )

    c1 = remote(g_ref.at[1 - c], r1, 0, partner)
    c1.start()
    ce1 = remote(e_ref, ebuf.at[0], 1, partner)
    ce1.start()
    c1.wait()
    ce1.wait()
    for j in range(4):
        s1[j] = g_ref[c, j] + r1[j]
    ebuf[1] = e_ref[...] + ebuf[0]

    done = []
    cr = cl = None
    for k in range(3):
        jr = (x + 3 - k) % 4
        jl = (x + k + 1) % 4
        if k == 0:
            src_r, src_l = s1.at[jr, 0], s1.at[jl, 1]
        else:
            cr.wait_recv()
            cl.wait_recv()
            acc_r[k] = s1[jr, 0] + recv_r[k - 1]
            acc_l[k] = s1[jl, 1] + recv_l[k - 1]
            src_r, src_l = acc_r.at[k], acc_l.at[k]
        cr = remote(src_r, recv_r.at[k], 2 + k, right)
        cr.start()
        cl = remote(src_l, recv_l.at[k], 5 + k, left)
        cl.start()
        done += [cr, cl]
        if k == 0:
            er = remote(ebuf.at[1], ebuf.at[2], 8, right)
            er.start()
            el = remote(ebuf.at[1], ebuf.at[3], 9, left)
            el.start()
            done += [er, el]
        if k == 1:
            er.wait_recv()
            ef = remote(ebuf.at[2], ebuf.at[4], 10, right)
            ef.start()
            done.append(ef)
    cr.wait_recv()
    cl.wait_recv()
    tbuf[0] = s1[x, 0] + recv_r[2]
    tbuf[1] = s1[x, 1] + recv_l[2]
    el.wait_recv()
    ef.wait_recv()
    ebuf[5] = ebuf[1] + ebuf[2] + ebuf[3] + ebuf[4]

    c3 = remote(tbuf.at[1 - yl], r3, 11, ypart)
    c3.start()
    ce3 = remote(ebuf.at[5], ebuf.at[6], 12, ypart)
    ce3.start()
    c3.wait()
    ce3.wait()
    out_ref[...] = tbuf[yl] + r3[...]
    eout_ref[...] = ebuf[5] + ebuf[6]
    for d in done:
        d.wait_send()


def scatter_grams(grams, energy_part):
    slots, rows, block = grams.shape[-3:]
    part = (slots, rows, block)
    f32 = jnp.float32
    return pl.pallas_call(
        scatter_kernel,
        out_shape=(
            jax.ShapeDtypeStruct(part, f32),
            jax.ShapeDtypeStruct(energy_part.shape, f32),
        ),
        in_specs=[pl.BlockSpec(memory_space=pltpu.VMEM)] * 2,
        out_specs=(pl.BlockSpec(memory_space=pltpu.VMEM),) * 2,
        scratch_shapes=[
            pltpu.VMEM((4, 2) + part, f32),
            pltpu.VMEM((4, 2) + part, f32),
            pltpu.VMEM((3,) + part, f32),
            pltpu.VMEM((3,) + part, f32),
            pltpu.VMEM((3,) + part, f32),
            pltpu.VMEM((3,) + part, f32),
            pltpu.VMEM((2,) + part, f32),
            pltpu.VMEM(part, f32),
            pltpu.VMEM((7,) + energy_part.shape, f32),
            pltpu.SemaphoreType.DMA((13,)),
            pltpu.SemaphoreType.DMA((13,)),
        ],
        compiler_params=pltpu.CompilerParams(
            collective_id=0, has_side_effects=True, vmem_limit_bytes=48 * 1024 * 1024
        ),
    )(grams, energy_part)


def on_device(images, stencil, pairs, live, rule_of_block, adduct):
    local_rows, pix_local = images.shape
    block = adduct.shape[1]
    local_blocks = local_rows // block
    shares = lax.axis_size("pix")
    rows = block // shares
    padded = extended_2(images, (("pix", 1),), 2)
    total = jnp.zeros((local_rows, pix_local), jnp.float32)
    for tap in range(5):
        total = total + stencil[tap][None, :] * padded[:, tap : tap + pix_local].astype(jnp.float32)
    smoothed = total.astype(jnp.bfloat16)
    extended = extended_2(smoothed, (("ion", 0),), REACH * block)
    values = extended.astype(jnp.float32)
    squares = jnp.sum(values * values, axis=1)
    pixel_count = pix_local * shares
    lookup_tables = lax.all_gather(adduct, "ion", axis=0, tiled=True)
    first = lax.axis_index("ion") * local_blocks
    slots = pairs.shape[0]
    relative = pairs - first + REACH

    grams = pair_grams(relative, extended, shares, block)
    gram, energy_sum = scatter_grams(grams, squares.reshape(-1, block))
    inverse = 1.0 / jnp.sqrt(energy_sum.reshape(-1) / pixel_count + 1e-06)
    inv_blocks = inverse.reshape(local_blocks + 2 * REACH, block)

    offset = lax.axis_index("pix") * rows
    inv_left = lax.dynamic_slice_in_dim(
        jnp.take(inv_blocks, relative[:, 0], axis=0), offset, rows, 1
    )
    inv_right = jnp.take(inv_blocks, relative[:, 1], axis=0)
    rules = jnp.take(rule_of_block, pairs[:, 1], axis=0)
    matrices = jnp.take(lookup_tables, rules, axis=0)
    coloc = (gram * inv_left[:, :, None] * inv_right[:, None, :] / pixel_count).astype(jnp.bfloat16)
    scores = jnp.einsum("src,scd->srd", coloc, matrices, preferred_element_type=jnp.float32)
    used = jnp.arange(slots, dtype=jnp.int32) < live[0]
    scores = jnp.where(used[:, None, None], scores, 0.0).astype(jnp.bfloat16)
    return (smoothed, scores)


def solution(mesh):
    return jax.shard_map(
        on_device,
        mesh=mesh,
        in_specs=(
            P("ion", "pix"),
            P(None, "pix"),
            P("ion", None),
            P("ion"),
            P(),
            P("ion", None, None),
        ),
        out_specs=(P("ion", "pix"), P("ion", "pix", None)),
        check_vma=False,
    )
```

```python
import jax
import jax.numpy as jnp
from jax import lax
from jax.experimental import pallas as pl
from jax.experimental.pallas import tpu as pltpu
from jax.sharding import PartitionSpec as P

REACH = 3


def extended_2(array, sides, width):
    for axis, dim in sides:
        size, length = (lax.axis_size(axis), array.shape[dim])
        up = [(i, (i + 1) % size) for i in range(size - 1)]
        down = [(j, i) for i, j in up]
        last = lax.slice_in_dim(array, length - width, length, axis=dim)
        first = lax.slice_in_dim(array, 0, width, axis=dim)
        before = lax.ppermute(last, axis, up)
        after = lax.ppermute(first, axis, down)
        array = jnp.concatenate([before, array, after], axis=dim)
    return array


def gram_kernel(shares, rel_ref, ext_ref, out_ref):
    block = out_ref.shape[-1]
    slots = out_ref.shape[-3]
    rows = out_ref.shape[-2]

    def body(s, carry):
        ra = rel_ref[2 * s]
        rb = rel_ref[2 * s + 1]
        left = ext_ref[pl.ds(pl.multiple_of(ra * block, block), block), :]
        right = ext_ref[pl.ds(pl.multiple_of(rb * block, block), block), :]
        g = lax.dot_general(
            left, right, (((1,), (1,)), ((), ())), preferred_element_type=jnp.float32
        )
        for q in range(shares):
            out_ref[q % 2, (q // 2) % 4, q // 8, s] = g[q * rows : (q + 1) * rows, :]
        return carry

    lax.fori_loop(0, slots, body, 0)


def pair_grams(relative, extended, shares, block):
    slots = relative.shape[0]
    rows = block // shares
    pix_local = extended.shape[1]
    flat = relative.reshape(-1).astype(jnp.int32)
    return pl.pallas_call(
        lambda *refs: gram_kernel(shares, *refs),
        out_shape=jax.ShapeDtypeStruct((2, 4, 2, slots, rows, block), jnp.float32),
        in_specs=[
            pl.BlockSpec(memory_space=pltpu.SMEM),
            pl.BlockSpec(memory_space=pltpu.VMEM),
        ],
        out_specs=pl.BlockSpec(memory_space=pltpu.VMEM),
        compiler_params=pltpu.CompilerParams(vmem_limit_bytes=48 * 1024 * 1024),
        cost_estimate=pl.CostEstimate(
            flops=2 * slots * block * block * pix_local,
            transcendentals=0,
            bytes_accessed=extended.size * 2 + slots * block * block * 4,
        ),
    )(flat, extended)


MESH = pl.DeviceIdType.MESH


def scatter_kernel(g_ref, e_ref, out_ref, eout_ref, r1, s1, recv_r, recv_l, acc_r, acc_l, tbuf, r3, ebuf, send_sem, recv_sem):
    p = lax.axis_index("pix")
    c = p % 2
    x = (p // 2) % 4
    yl = p // 8
    partner = p + 1 - 2 * c
    right = (yl * 4 + (x + 1) % 4) * 2 + c
    left = (yl * 4 + (x + 3) % 4) * 2 + c
    ypart = ((1 - yl) * 4 + x) * 2 + c

    barrier = pltpu.get_barrier_semaphore()
    for peer in (partner, right, left, ypart):
        pl.semaphore_signal(barrier, 1, device_id={"pix": peer}, device_id_type=MESH)
    pl.semaphore_wait(barrier, 4)

    def remote(src, dst, k, peer):
        return pltpu.make_async_remote_copy(
            src_ref=src, dst_ref=dst, send_sem=send_sem.at[k], recv_sem=recv_sem.at[k],
            device_id={"pix": peer}, device_id_type=MESH,
        )

    c1 = remote(g_ref.at[1 - c], r1, 0, partner)
    c1.start()
    ce1 = remote(e_ref, ebuf.at[0], 1, partner)
    ce1.start()
    c1.wait()
    ce1.wait()
    for j in range(4):
        s1[j] = g_ref[c, j] + r1[j]
    ebuf[1] = e_ref[...] + ebuf[0]

    done = []
    cr = cl = None
    for k in range(3):
        jr = (x + 3 - k) % 4
        jl = (x + k + 1) % 4
        if k == 0:
            src_r, src_l = s1.at[jr, 0], s1.at[jl, 1]
        else:
            cr.wait_recv()
            cl.wait_recv()
            acc_r[k] = s1[jr, 0] + recv_r[k - 1]
            acc_l[k] = s1[jl, 1] + recv_l[k - 1]
            src_r, src_l = acc_r.at[k], acc_l.at[k]
        cr = remote(src_r, recv_r.at[k], 2 + k, right)
        cr.start()
        cl = remote(src_l, recv_l.at[k], 5 + k, left)
        cl.start()
        done += [cr, cl]
        if k == 0:
            er = remote(ebuf.at[1], ebuf.at[2], 8, right)
            er.start()
            el = remote(ebuf.at[1], ebuf.at[3], 9, left)
            el.start()
            done += [er, el]
        if k == 1:
            er.wait_recv()
            ef = remote(ebuf.at[2], ebuf.at[4], 10, right)
            ef.start()
            done.append(ef)
    cr.wait_recv()
    cl.wait_recv()
    tbuf[0] = s1[x, 0] + recv_r[2]
    tbuf[1] = s1[x, 1] + recv_l[2]
    el.wait_recv()
    ef.wait_recv()
    ebuf[5] = ebuf[1] + ebuf[2] + ebuf[3] + ebuf[4]

    c3 = remote(tbuf.at[1 - yl], r3, 11, ypart)
    c3.start()
    ce3 = remote(ebuf.at[5], ebuf.at[6], 12, ypart)
    ce3.start()
    c3.wait()
    ce3.wait()
    out_ref[...] = tbuf[yl] + r3[...]
    eout_ref[...] = ebuf[5] + ebuf[6]
    for d in done:
        d.wait_send()


def scatter_grams(grams, energy_part):
    slots, rows, block = grams.shape[-3:]
    part = (slots, rows, block)
    f32 = jnp.float32
    return pl.pallas_call(
        scatter_kernel,
        out_shape=(
            jax.ShapeDtypeStruct(part, f32),
            jax.ShapeDtypeStruct(energy_part.shape, f32),
        ),
        in_specs=[pl.BlockSpec(memory_space=pltpu.VMEM)] * 2,
        out_specs=(pl.BlockSpec(memory_space=pltpu.VMEM),) * 2,
        scratch_shapes=[
            pltpu.VMEM((4, 2) + part, f32),
            pltpu.VMEM((4, 2) + part, f32),
            pltpu.VMEM((3,) + part, f32),
            pltpu.VMEM((3,) + part, f32),
            pltpu.VMEM((3,) + part, f32),
            pltpu.VMEM((3,) + part, f32),
            pltpu.VMEM((2,) + part, f32),
            pltpu.VMEM(part, f32),
            pltpu.VMEM((7,) + energy_part.shape, f32),
            pltpu.SemaphoreType.DMA((13,)),
            pltpu.SemaphoreType.DMA((13,)),
        ],
        compiler_params=pltpu.CompilerParams(
            collective_id=0, has_side_effects=True, vmem_limit_bytes=48 * 1024 * 1024
        ),
    )(grams, energy_part)


def smooth_rows(padded, stencil):
    pix_local = stencil.shape[1]
    total = jnp.zeros((padded.shape[0], pix_local), jnp.float32)
    for tap in range(5):
        total = total + stencil[tap][None, :] * padded[:, tap : tap + pix_local].astype(jnp.float32)
    return total.astype(jnp.bfloat16)


def row_squares(rows):
    values = rows.astype(jnp.float32)
    return jnp.sum(values * values, axis=1)


def on_device(images, stencil, pairs, live, rule_of_block, adduct):
    local_rows, pix_local = images.shape
    block = adduct.shape[1]
    local_blocks = local_rows // block
    shares = lax.axis_size("pix")
    rows = block // shares
    width = REACH * block
    ions = lax.axis_size("ion")
    up = [(i, i + 1) for i in range(ions - 1)]
    down = [(j, i) for i, j in up]
    raw_before = lax.ppermute(images[local_rows - width :], "ion", up)
    raw_after = lax.ppermute(images[:width], "ion", down)
    offset = lax.axis_index("pix") * rows
    piece = lax.dynamic_slice_in_dim(adduct, offset, rows, 1)
    lookup_tables = lax.all_gather(
        lax.all_gather(piece, "ion", axis=0, tiled=True), "pix", axis=1, tiled=True
    )
    padded = extended_2(images, (("pix", 1),), 2)
    smoothed = smooth_rows(padded, stencil)
    local_squares = row_squares(smoothed)
    edges = jnp.concatenate([padded[:, :2], padded[:, pix_local + 2 :]], axis=1)
    edge_before = lax.ppermute(edges[local_rows - width :], "ion", up)
    edge_after = lax.ppermute(edges[:width], "ion", down)
    before = smooth_rows(
        jnp.concatenate([edge_before[:, :2], raw_before, edge_before[:, 2:]], axis=1), stencil
    )
    after = smooth_rows(
        jnp.concatenate([edge_after[:, :2], raw_after, edge_after[:, 2:]], axis=1), stencil
    )
    extended = jnp.concatenate([before, smoothed, after], axis=0)
    squares = jnp.concatenate([row_squares(before), local_squares, row_squares(after)])
    pixel_count = pix_local * shares
    first = lax.axis_index("ion") * local_blocks
    slots = pairs.shape[0]
    relative = pairs - first + REACH

    grams = pair_grams(relative, extended, shares, block)
    gram, energy_sum = scatter_grams(grams, squares.reshape(-1, block))
    inverse = 1.0 / jnp.sqrt(energy_sum.reshape(-1) / pixel_count + 1e-06)
    inv_blocks = inverse.reshape(local_blocks + 2 * REACH, block)

    inv_left = lax.dynamic_slice_in_dim(
        jnp.take(inv_blocks, relative[:, 0], axis=0), offset, rows, 1
    )
    inv_right = jnp.take(inv_blocks, relative[:, 1], axis=0)
    rules = jnp.take(rule_of_block, pairs[:, 1], axis=0)
    matrices = jnp.take(lookup_tables, rules, axis=0)
    coloc = (gram * inv_left[:, :, None] * inv_right[:, None, :] / pixel_count).astype(jnp.bfloat16)
    scores = jnp.einsum("src,scd->srd", coloc, matrices, preferred_element_type=jnp.float32)
    used = jnp.arange(slots, dtype=jnp.int32) < live[0]
    scores = jnp.where(used[:, None, None], scores, 0.0).astype(jnp.bfloat16)
    return (smoothed, scores)


def solution(mesh):
    return jax.shard_map(
        on_device,
        mesh=mesh,
        in_specs=(
            P("ion", "pix"),
            P(None, "pix"),
            P("ion", None),
            P("ion"),
            P(),
            P("ion", None, None),
        ),
        out_specs=(P("ion", "pix"), P("ion", "pix", None)),
        check_vma=False,
    )
```

```python
import jax
import jax.numpy as jnp
from jax import lax
from jax.experimental import pallas as pl
from jax.experimental.pallas import tpu as pltpu
from jax.sharding import PartitionSpec as P

REACH = 3


def extended_2(array, sides, width):
    for axis, dim in sides:
        size, length = (lax.axis_size(axis), array.shape[dim])
        up = [(i, (i + 1) % size) for i in range(size - 1)]
        down = [(j, i) for i, j in up]
        last = lax.slice_in_dim(array, length - width, length, axis=dim)
        first = lax.slice_in_dim(array, 0, width, axis=dim)
        before = lax.ppermute(last, axis, up)
        after = lax.ppermute(first, axis, down)
        array = jnp.concatenate([before, array, after], axis=dim)
    return array


def gram_kernel(shares, rel_ref, ext_ref, out_ref):
    block = out_ref.shape[-1]
    slots = out_ref.shape[-3]
    rows = out_ref.shape[-2]

    def body(s, carry):
        ra = rel_ref[2 * s]
        rb = rel_ref[2 * s + 1]
        left = ext_ref[pl.ds(pl.multiple_of(ra * block, block), block), :]
        right = ext_ref[pl.ds(pl.multiple_of(rb * block, block), block), :]
        g = lax.dot_general(
            left, right, (((1,), (1,)), ((), ())), preferred_element_type=jnp.float32
        )
        for q in range(shares):
            out_ref[q % 2, (q // 2) % 4, q // 8, s] = g[q * rows : (q + 1) * rows, :]
        return carry

    lax.fori_loop(0, slots, body, 0)


def pair_grams(relative, extended, shares, block):
    slots = relative.shape[0]
    rows = block // shares
    pix_local = extended.shape[1]
    flat = relative.reshape(-1).astype(jnp.int32)
    return pl.pallas_call(
        lambda *refs: gram_kernel(shares, *refs),
        out_shape=jax.ShapeDtypeStruct((2, 4, 2, slots, rows, block), jnp.float32),
        in_specs=[
            pl.BlockSpec(memory_space=pltpu.SMEM),
            pl.BlockSpec(memory_space=pltpu.VMEM),
        ],
        out_specs=pl.BlockSpec(memory_space=pltpu.VMEM),
        compiler_params=pltpu.CompilerParams(vmem_limit_bytes=48 * 1024 * 1024),
        cost_estimate=pl.CostEstimate(
            flops=2 * slots * block * block * pix_local,
            transcendentals=0,
            bytes_accessed=extended.size * 2 + slots * block * block * 4,
        ),
    )(flat, extended)


MESH = pl.DeviceIdType.MESH


def scatter_kernel(g_ref, e_ref, out_ref, eout_ref, r1, s1, recv_r, recv_l, acc_r, acc_l, tbuf, r3, ebuf, send_sem, recv_sem):
    p = lax.axis_index("pix")
    c = p % 2
    x = (p // 2) % 4
    yl = p // 8
    partner = p + 1 - 2 * c
    right = (yl * 4 + (x + 1) % 4) * 2 + c
    left = (yl * 4 + (x + 3) % 4) * 2 + c
    ypart = ((1 - yl) * 4 + x) * 2 + c

    barrier = pltpu.get_barrier_semaphore()
    for peer in (partner, right, left, ypart):
        pl.semaphore_signal(barrier, 1, device_id={"pix": peer}, device_id_type=MESH)
    pl.semaphore_wait(barrier, 4)

    def remote(src, dst, k, peer):
        return pltpu.make_async_remote_copy(
            src_ref=src, dst_ref=dst, send_sem=send_sem.at[k], recv_sem=recv_sem.at[k],
            device_id={"pix": peer}, device_id_type=MESH,
        )

    c1 = remote(g_ref.at[1 - c], r1, 0, partner)
    c1.start()
    ce1 = remote(e_ref, ebuf.at[0], 1, partner)
    ce1.start()
    c1.wait()
    ce1.wait()
    for j in range(4):
        s1[j] = g_ref[c, j] + r1[j]
    ebuf[1] = e_ref[...] + ebuf[0]

    done = []
    cr = cl = None
    for k in range(3):
        jr = (x + 3 - k) % 4
        jl = (x + k + 1) % 4
        if k == 0:
            src_r, src_l = s1.at[jr, 0], s1.at[jl, 1]
        else:
            cr.wait_recv()
            cl.wait_recv()
            acc_r[k] = s1[jr, 0] + recv_r[k - 1]
            acc_l[k] = s1[jl, 1] + recv_l[k - 1]
            src_r, src_l = acc_r.at[k], acc_l.at[k]
        cr = remote(src_r, recv_r.at[k], 2 + k, right)
        cr.start()
        cl = remote(src_l, recv_l.at[k], 5 + k, left)
        cl.start()
        done += [cr, cl]
        if k == 0:
            er = remote(ebuf.at[1], ebuf.at[2], 8, right)
            er.start()
            el = remote(ebuf.at[1], ebuf.at[3], 9, left)
            el.start()
            done += [er, el]
        if k == 1:
            er.wait_recv()
            ef = remote(ebuf.at[2], ebuf.at[4], 10, right)
            ef.start()
            done.append(ef)
    cr.wait_recv()
    cl.wait_recv()
    tbuf[0] = s1[x, 0] + recv_r[2]
    tbuf[1] = s1[x, 1] + recv_l[2]
    el.wait_recv()
    ef.wait_recv()
    ebuf[5] = ebuf[1] + ebuf[2] + ebuf[3] + ebuf[4]

    c3 = remote(tbuf.at[1 - yl], r3, 11, ypart)
    c3.start()
    ce3 = remote(ebuf.at[5], ebuf.at[6], 12, ypart)
    ce3.start()
    c3.wait()
    ce3.wait()
    out_ref[...] = tbuf[yl] + r3[...]
    eout_ref[...] = ebuf[5] + ebuf[6]
    for d in done:
        d.wait_send()


def scatter_grams(grams, energy_part):
    slots, rows, block = grams.shape[-3:]
    part = (slots, rows, block)
    f32 = jnp.float32
    return pl.pallas_call(
        scatter_kernel,
        out_shape=(
            jax.ShapeDtypeStruct(part, f32),
            jax.ShapeDtypeStruct(energy_part.shape, f32),
        ),
        in_specs=[pl.BlockSpec(memory_space=pltpu.VMEM)] * 2,
        out_specs=(pl.BlockSpec(memory_space=pltpu.VMEM),) * 2,
        scratch_shapes=[
            pltpu.VMEM((4, 2) + part, f32),
            pltpu.VMEM((4, 2) + part, f32),
            pltpu.VMEM((3,) + part, f32),
            pltpu.VMEM((3,) + part, f32),
            pltpu.VMEM((3,) + part, f32),
            pltpu.VMEM((3,) + part, f32),
            pltpu.VMEM((2,) + part, f32),
            pltpu.VMEM(part, f32),
            pltpu.VMEM((7,) + energy_part.shape, f32),
            pltpu.SemaphoreType.DMA((13,)),
            pltpu.SemaphoreType.DMA((13,)),
        ],
        compiler_params=pltpu.CompilerParams(
            collective_id=0, has_side_effects=True, vmem_limit_bytes=48 * 1024 * 1024
        ),
    )(grams, energy_part)


def smooth_rows(padded, stencil):
    pix_local = stencil.shape[1]
    total = jnp.zeros((padded.shape[0], pix_local), jnp.float32)
    for tap in range(5):
        total = total + stencil[tap][None, :] * padded[:, tap : tap + pix_local].astype(jnp.float32)
    return total.astype(jnp.bfloat16)


def row_squares(rows):
    values = rows.astype(jnp.float32)
    return jnp.sum(values * values, axis=1)


def on_device(images, stencil, pairs, live, rule_of_block, adduct):
    local_rows, pix_local = images.shape
    block = adduct.shape[1]
    local_blocks = local_rows // block
    shares = lax.axis_size("pix")
    rows = block // shares
    width = REACH * block
    ions = lax.axis_size("ion")
    up = [(i, i + 1) for i in range(ions - 1)]
    down = [(j, i) for i, j in up]
    raw_before = lax.ppermute(images[local_rows - width :], "ion", up)
    raw_after = lax.ppermute(images[:width], "ion", down)
    me_pix = lax.axis_index("pix")
    me_ion = lax.axis_index("ion")
    offset = me_pix * rows
    turn = [
        (p * ions + j, p * ions + (j - p) % ions)
        for j in range(ions)
        for p in range(1, shares)
    ]
    fetched = lax.ppermute(adduct, ("pix", "ion"), turn)
    own_turn = jnp.where(me_pix == 0, adduct, fetched)
    lookup_tables = lax.all_gather(own_turn, "pix", axis=0, tiled=True)
    padded = extended_2(images, (("pix", 1),), 2)
    smoothed = smooth_rows(padded, stencil)
    local_squares = row_squares(smoothed)
    edges = jnp.concatenate([padded[:, :2], padded[:, pix_local + 2 :]], axis=1)
    edge_before = lax.ppermute(edges[local_rows - width :], "ion", up)
    edge_after = lax.ppermute(edges[:width], "ion", down)
    before = smooth_rows(
        jnp.concatenate([edge_before[:, :2], raw_before, edge_before[:, 2:]], axis=1), stencil
    )
    after = smooth_rows(
        jnp.concatenate([edge_after[:, :2], raw_after, edge_after[:, 2:]], axis=1), stencil
    )
    extended = jnp.concatenate([before, smoothed, after], axis=0)
    squares = jnp.concatenate([row_squares(before), local_squares, row_squares(after)])
    pixel_count = pix_local * shares
    first = lax.axis_index("ion") * local_blocks
    slots = pairs.shape[0]
    relative = pairs - first + REACH

    grams = pair_grams(relative, extended, shares, block)
    gram, energy_sum = scatter_grams(grams, squares.reshape(-1, block))
    inverse = 1.0 / jnp.sqrt(energy_sum.reshape(-1) / pixel_count + 1e-06)
    inv_blocks = inverse.reshape(local_blocks + 2 * REACH, block)

    inv_left = lax.dynamic_slice_in_dim(
        jnp.take(inv_blocks, relative[:, 0], axis=0), offset, rows, 1
    )
    inv_right = jnp.take(inv_blocks, relative[:, 1], axis=0)
    rules = jnp.take(rule_of_block, pairs[:, 1], axis=0)
    per_index = adduct.shape[0]
    rules = ((rules // per_index - me_ion) % ions) * per_index + rules % per_index
    matrices = jnp.take(lookup_tables, rules, axis=0)
    coloc = (gram * inv_left[:, :, None] * inv_right[:, None, :] / pixel_count).astype(jnp.bfloat16)
    scores = jnp.einsum("src,scd->srd", coloc, matrices, preferred_element_type=jnp.float32)
    used = jnp.arange(slots, dtype=jnp.int32) < live[0]
    scores = jnp.where(used[:, None, None], scores, 0.0).astype(jnp.bfloat16)
    return (smoothed, scores)


def solution(mesh):
    return jax.shard_map(
        on_device,
        mesh=mesh,
        in_specs=(
            P("ion", "pix"),
            P(None, "pix"),
            P("ion", None),
            P("ion"),
            P(),
            P("ion", None, None),
        ),
        out_specs=(P("ion", "pix"), P("ion", "pix", None)),
        check_vma=False,
    )
```

```python
import jax
import jax.numpy as jnp
from jax import lax
from jax.experimental import pallas as pl
from jax.experimental.pallas import tpu as pltpu
from jax.sharding import PartitionSpec as P

REACH = 3


def extended_2(array, sides, width):
    for axis, dim in sides:
        size, length = (lax.axis_size(axis), array.shape[dim])
        up = [(i, (i + 1) % size) for i in range(size - 1)]
        down = [(j, i) for i, j in up]
        last = lax.slice_in_dim(array, length - width, length, axis=dim)
        first = lax.slice_in_dim(array, 0, width, axis=dim)
        before = lax.ppermute(last, axis, up)
        after = lax.ppermute(first, axis, down)
        array = jnp.concatenate([before, array, after], axis=dim)
    return array


def gram_kernel(shares, rel_ref, before_ref, local_ref, after_ref, out_ref, ext_ref, sems):
    block = out_ref.shape[-1]
    slots = out_ref.shape[-3]
    rows = out_ref.shape[-2]
    width = before_ref.shape[0]
    middle = local_ref.shape[0]
    copies = [
        pltpu.make_async_copy(local_ref, ext_ref.at[pl.ds(width, middle)], sems.at[0]),
        pltpu.make_async_copy(before_ref, ext_ref.at[pl.ds(0, width)], sems.at[1]),
        pltpu.make_async_copy(after_ref, ext_ref.at[pl.ds(width + middle, width)], sems.at[2]),
    ]
    for cp in copies:
        cp.start()
    for cp in copies:
        cp.wait()

    def body(s, carry):
        ra = rel_ref[2 * s]
        rb = rel_ref[2 * s + 1]
        left = ext_ref[pl.ds(pl.multiple_of(ra * block, block), block), :]
        right = ext_ref[pl.ds(pl.multiple_of(rb * block, block), block), :]
        g = lax.dot_general(
            left, right, (((1,), (1,)), ((), ())), preferred_element_type=jnp.float32
        )
        for q in range(shares):
            out_ref[q % 2, (q // 2) % 4, q // 8, s] = g[q * rows : (q + 1) * rows, :]
        return carry

    lax.fori_loop(0, slots, body, 0)


def pair_grams(relative, before, local, after, shares, block):
    slots = relative.shape[0]
    rows = block // shares
    pix_local = local.shape[1]
    ext_rows = before.shape[0] + local.shape[0] + after.shape[0]
    flat = relative.reshape(-1).astype(jnp.int32)
    return pl.pallas_call(
        lambda *refs: gram_kernel(shares, *refs),
        out_shape=jax.ShapeDtypeStruct((2, 4, 2, slots, rows, block), jnp.float32),
        in_specs=[pl.BlockSpec(memory_space=pltpu.SMEM)]
        + [pl.BlockSpec(memory_space=pl.ANY)] * 3,
        out_specs=pl.BlockSpec(memory_space=pltpu.VMEM),
        scratch_shapes=[
            pltpu.VMEM((ext_rows, pix_local), local.dtype),
            pltpu.SemaphoreType.DMA((3,)),
        ],
        compiler_params=pltpu.CompilerParams(vmem_limit_bytes=48 * 1024 * 1024),
        cost_estimate=pl.CostEstimate(
            flops=2 * slots * block * block * pix_local,
            transcendentals=0,
            bytes_accessed=ext_rows * pix_local * 2 + slots * block * block * 4,
        ),
    )(flat, before, local, after)

MESH = pl.DeviceIdType.MESH


def scatter_kernel(g_ref, e_ref, out_ref, eout_ref, r1, s1, recv_r, recv_l, acc_r, acc_l, tbuf, r3, ebuf, send_sem, recv_sem):
    p = lax.axis_index("pix")
    c = p % 2
    x = (p // 2) % 4
    yl = p // 8
    partner = p + 1 - 2 * c
    right = (yl * 4 + (x + 1) % 4) * 2 + c
    left = (yl * 4 + (x + 3) % 4) * 2 + c
    ypart = ((1 - yl) * 4 + x) * 2 + c

    barrier = pltpu.get_barrier_semaphore()
    for peer in (partner, right, left, ypart):
        pl.semaphore_signal(barrier, 1, device_id={"pix": peer}, device_id_type=MESH)
    pl.semaphore_wait(barrier, 4)

    def remote(src, dst, k, peer):
        return pltpu.make_async_remote_copy(
            src_ref=src, dst_ref=dst, send_sem=send_sem.at[k], recv_sem=recv_sem.at[k],
            device_id={"pix": peer}, device_id_type=MESH,
        )

    c1 = remote(g_ref.at[1 - c], r1, 0, partner)
    c1.start()
    ce1 = remote(e_ref, ebuf.at[0], 1, partner)
    ce1.start()
    c1.wait()
    ce1.wait()
    for j in range(4):
        s1[j] = g_ref[c, j] + r1[j]
    ebuf[1] = e_ref[...] + ebuf[0]

    done = []
    cr = cl = None
    for k in range(3):
        jr = (x + 3 - k) % 4
        jl = (x + k + 1) % 4
        if k == 0:
            src_r, src_l = s1.at[jr, 0], s1.at[jl, 1]
        else:
            cr.wait_recv()
            cl.wait_recv()
            acc_r[k] = s1[jr, 0] + recv_r[k - 1]
            acc_l[k] = s1[jl, 1] + recv_l[k - 1]
            src_r, src_l = acc_r.at[k], acc_l.at[k]
        cr = remote(src_r, recv_r.at[k], 2 + k, right)
        cr.start()
        cl = remote(src_l, recv_l.at[k], 5 + k, left)
        cl.start()
        done += [cr, cl]
        if k == 0:
            er = remote(ebuf.at[1], ebuf.at[2], 8, right)
            er.start()
            el = remote(ebuf.at[1], ebuf.at[3], 9, left)
            el.start()
            done += [er, el]
        if k == 1:
            er.wait_recv()
            ef = remote(ebuf.at[2], ebuf.at[4], 10, right)
            ef.start()
            done.append(ef)
    cr.wait_recv()
    cl.wait_recv()
    tbuf[0] = s1[x, 0] + recv_r[2]
    tbuf[1] = s1[x, 1] + recv_l[2]
    el.wait_recv()
    ef.wait_recv()
    ebuf[5] = ebuf[1] + ebuf[2] + ebuf[3] + ebuf[4]

    c3 = remote(tbuf.at[1 - yl], r3, 11, ypart)
    c3.start()
    ce3 = remote(ebuf.at[5], ebuf.at[6], 12, ypart)
    ce3.start()
    c3.wait()
    ce3.wait()
    out_ref[...] = tbuf[yl] + r3[...]
    eout_ref[...] = ebuf[5] + ebuf[6]
    for d in done:
        d.wait_send()


def scatter_grams(grams, energy_part):
    slots, rows, block = grams.shape[-3:]
    part = (slots, rows, block)
    f32 = jnp.float32
    return pl.pallas_call(
        scatter_kernel,
        out_shape=(
            jax.ShapeDtypeStruct(part, f32),
            jax.ShapeDtypeStruct(energy_part.shape, f32),
        ),
        in_specs=[pl.BlockSpec(memory_space=pltpu.VMEM)] * 2,
        out_specs=(pl.BlockSpec(memory_space=pltpu.VMEM),) * 2,
        scratch_shapes=[
            pltpu.VMEM((4, 2) + part, f32),
            pltpu.VMEM((4, 2) + part, f32),
            pltpu.VMEM((3,) + part, f32),
            pltpu.VMEM((3,) + part, f32),
            pltpu.VMEM((3,) + part, f32),
            pltpu.VMEM((3,) + part, f32),
            pltpu.VMEM((2,) + part, f32),
            pltpu.VMEM(part, f32),
            pltpu.VMEM((7,) + energy_part.shape, f32),
            pltpu.SemaphoreType.DMA((13,)),
            pltpu.SemaphoreType.DMA((13,)),
        ],
        compiler_params=pltpu.CompilerParams(
            collective_id=0, has_side_effects=True, vmem_limit_bytes=48 * 1024 * 1024
        ),
    )(grams, energy_part)


def smooth_rows(padded, stencil):
    pix_local = stencil.shape[1]
    total = jnp.zeros((padded.shape[0], pix_local), jnp.float32)
    for tap in range(5):
        total = total + stencil[tap][None, :] * padded[:, tap : tap + pix_local].astype(jnp.float32)
    return total.astype(jnp.bfloat16)


def row_squares(rows):
    values = rows.astype(jnp.float32)
    return jnp.sum(values * values, axis=1)


def on_device(images, stencil, pairs, live, rule_of_block, adduct):
    local_rows, pix_local = images.shape
    block = adduct.shape[1]
    local_blocks = local_rows // block
    shares = lax.axis_size("pix")
    rows = block // shares
    width = REACH * block
    ions = lax.axis_size("ion")
    up = [(i, i + 1) for i in range(ions - 1)]
    down = [(j, i) for i, j in up]
    raw_before = lax.ppermute(images[local_rows - width :], "ion", up)
    raw_after = lax.ppermute(images[:width], "ion", down)
    me_pix = lax.axis_index("pix")
    offset = me_pix * rows
    lookup_tables = lax.all_gather(adduct, "ion", axis=0, tiled=True)
    padded = extended_2(images, (("pix", 1),), 2)
    smoothed = smooth_rows(padded, stencil)
    local_squares = row_squares(smoothed)
    edges = jnp.concatenate([padded[:, :2], padded[:, pix_local + 2 :]], axis=1)
    edge_before = lax.ppermute(edges[local_rows - width :], "ion", up)
    edge_after = lax.ppermute(edges[:width], "ion", down)
    before = smooth_rows(
        jnp.concatenate([edge_before[:, :2], raw_before, edge_before[:, 2:]], axis=1), stencil
    )
    after = smooth_rows(
        jnp.concatenate([edge_after[:, :2], raw_after, edge_after[:, 2:]], axis=1), stencil
    )
    squares = jnp.concatenate([row_squares(before), local_squares, row_squares(after)])
    pixel_count = pix_local * shares
    first = lax.axis_index("ion") * local_blocks
    slots = pairs.shape[0]
    relative = pairs - first + REACH

    grams = pair_grams(relative, before, smoothed, after, shares, block)
    gram, energy_sum = scatter_grams(grams, squares.reshape(-1, block))
    inverse = 1.0 / jnp.sqrt(energy_sum.reshape(-1) / pixel_count + 1e-06)
    inv_blocks = inverse.reshape(local_blocks + 2 * REACH, block)

    inv_left = lax.dynamic_slice_in_dim(
        jnp.take(inv_blocks, relative[:, 0], axis=0), offset, rows, 1
    )
    inv_right = jnp.take(inv_blocks, relative[:, 1], axis=0)
    rules = jnp.take(rule_of_block, pairs[:, 1], axis=0)
    matrices = jnp.take(lookup_tables, rules, axis=0)
    coloc = (gram * inv_left[:, :, None] * inv_right[:, None, :] / pixel_count).astype(jnp.bfloat16)
    scores = jnp.einsum("src,scd->srd", coloc, matrices, preferred_element_type=jnp.float32)
    used = jnp.arange(slots, dtype=jnp.int32) < live[0]
    scores = jnp.where(used[:, None, None], scores, 0.0).astype(jnp.bfloat16)
    return (smoothed, scores)


def solution(mesh):
    return jax.shard_map(
        on_device,
        mesh=mesh,
        in_specs=(
            P("ion", "pix"),
            P(None, "pix"),
            P("ion", None),
            P("ion"),
            P(),
            P("ion", None, None),
        ),
        out_specs=(P("ion", "pix"), P("ion", "pix", None)),
        check_vma=False,
    )
```

```python
import jax
import jax.numpy as jnp
from jax import lax
from jax.experimental import pallas as pl
from jax.experimental.pallas import tpu as pltpu
from jax.sharding import PartitionSpec as P

REACH = 3


def extended_2(array, sides, width):
    for axis, dim in sides:
        size, length = (lax.axis_size(axis), array.shape[dim])
        up = [(i, (i + 1) % size) for i in range(size - 1)]
        down = [(j, i) for i, j in up]
        last = lax.slice_in_dim(array, length - width, length, axis=dim)
        first = lax.slice_in_dim(array, 0, width, axis=dim)
        before = lax.ppermute(last, axis, up)
        after = lax.ppermute(first, axis, down)
        array = jnp.concatenate([before, array, after], axis=dim)
    return array


def gram_kernel(shares, rel_ref, before_ref, local_ref, after_ref, out_ref, ext_ref, sems):
    block = out_ref.shape[-1]
    slots = out_ref.shape[-3]
    rows = out_ref.shape[-2]
    width = before_ref.shape[0]
    middle = local_ref.shape[0]
    copies = [
        pltpu.make_async_copy(local_ref, ext_ref.at[pl.ds(width, middle)], sems.at[0]),
        pltpu.make_async_copy(before_ref, ext_ref.at[pl.ds(0, width)], sems.at[1]),
        pltpu.make_async_copy(after_ref, ext_ref.at[pl.ds(width + middle, width)], sems.at[2]),
    ]
    for cp in copies:
        cp.start()
    for cp in copies:
        cp.wait()

    def body(s, carry):
        ra = rel_ref[2 * s]
        rb = rel_ref[2 * s + 1]
        left = ext_ref[pl.ds(pl.multiple_of(ra * block, block), block), :]
        right = ext_ref[pl.ds(pl.multiple_of(rb * block, block), block), :]
        g = lax.dot_general(
            left, right, (((1,), (1,)), ((), ())), preferred_element_type=jnp.float32
        )
        for q in range(shares):
            out_ref[q % 2, (q // 2) % 4, q // 8, s] = g[q * rows : (q + 1) * rows, :]
        return carry

    lax.fori_loop(0, slots, body, 0)


def pair_grams(relative, before, local, after, shares, block):
    slots = relative.shape[0]
    rows = block // shares
    pix_local = local.shape[1]
    ext_rows = before.shape[0] + local.shape[0] + after.shape[0]
    flat = relative.reshape(-1).astype(jnp.int32)
    return pl.pallas_call(
        lambda *refs: gram_kernel(shares, *refs),
        out_shape=jax.ShapeDtypeStruct((2, 4, 2, slots, rows, block), jnp.float32),
        in_specs=[pl.BlockSpec(memory_space=pltpu.SMEM)]
        + [pl.BlockSpec(memory_space=pl.ANY)] * 3,
        out_specs=pl.BlockSpec(memory_space=pltpu.VMEM),
        scratch_shapes=[
            pltpu.VMEM((ext_rows, pix_local), local.dtype),
            pltpu.SemaphoreType.DMA((3,)),
        ],
        compiler_params=pltpu.CompilerParams(vmem_limit_bytes=48 * 1024 * 1024),
        cost_estimate=pl.CostEstimate(
            flops=2 * slots * block * block * pix_local,
            transcendentals=0,
            bytes_accessed=ext_rows * pix_local * 2 + slots * block * block * 4,
        ),
    )(flat, before, local, after)

MESH = pl.DeviceIdType.MESH


def scatter_kernel(g_ref, e_ref, out_ref, eout_ref, r1, s1, recv_r, recv_l, acc_r, acc_l, tbuf, r3, ebuf, send_sem, recv_sem):
    p = lax.axis_index("pix")
    c = p % 2
    x = (p // 2) % 4
    yl = p // 8
    partner = p + 1 - 2 * c
    right = (yl * 4 + (x + 1) % 4) * 2 + c
    left = (yl * 4 + (x + 3) % 4) * 2 + c
    ypart = ((1 - yl) * 4 + x) * 2 + c

    barrier = pltpu.get_barrier_semaphore()
    for peer in (partner, right, left, ypart):
        pl.semaphore_signal(barrier, 1, device_id={"pix": peer}, device_id_type=MESH)
    pl.semaphore_wait(barrier, 4)

    def remote(src, dst, k, peer):
        return pltpu.make_async_remote_copy(
            src_ref=src, dst_ref=dst, send_sem=send_sem.at[k], recv_sem=recv_sem.at[k],
            device_id={"pix": peer}, device_id_type=MESH,
        )

    c1 = remote(g_ref.at[1 - c], r1, 0, partner)
    c1.start()
    ce1 = remote(e_ref, ebuf.at[0], 1, partner)
    ce1.start()
    c1.wait()
    ce1.wait()
    for j in range(4):
        s1[j] = g_ref[c, j] + r1[j]
    ebuf[1] = e_ref[...] + ebuf[0]

    done = []
    cr = cl = None
    for k in range(3):
        jr = (x + 3 - k) % 4
        jl = (x + k + 1) % 4
        if k == 0:
            src_r, src_l = s1.at[jr, 0], s1.at[jl, 1]
        else:
            cr.wait_recv()
            cl.wait_recv()
            acc_r[k] = s1[jr, 0] + recv_r[k - 1]
            acc_l[k] = s1[jl, 1] + recv_l[k - 1]
            src_r, src_l = acc_r.at[k], acc_l.at[k]
        cr = remote(src_r, recv_r.at[k], 2 + k, right)
        cr.start()
        cl = remote(src_l, recv_l.at[k], 5 + k, left)
        cl.start()
        done += [cr, cl]
        if k == 0:
            er = remote(ebuf.at[1], ebuf.at[2], 8, right)
            er.start()
            el = remote(ebuf.at[1], ebuf.at[3], 9, left)
            el.start()
            done += [er, el]
        if k == 1:
            er.wait_recv()
            ef = remote(ebuf.at[2], ebuf.at[4], 10, right)
            ef.start()
            done.append(ef)
    cr.wait_recv()
    cl.wait_recv()
    tbuf[0] = s1[x, 0] + recv_r[2]
    tbuf[1] = s1[x, 1] + recv_l[2]
    el.wait_recv()
    ef.wait_recv()
    ebuf[5] = ebuf[1] + ebuf[2] + ebuf[3] + ebuf[4]

    c3 = remote(tbuf.at[1 - yl], r3, 11, ypart)
    c3.start()
    ce3 = remote(ebuf.at[5], ebuf.at[6], 12, ypart)
    ce3.start()
    c3.wait()
    ce3.wait()
    out_ref[...] = tbuf[yl] + r3[...]
    eout_ref[...] = ebuf[5] + ebuf[6]
    for d in done:
        d.wait_send()


def scatter_grams(grams, energy_part):
    slots, rows, block = grams.shape[-3:]
    part = (slots, rows, block)
    f32 = jnp.float32
    return pl.pallas_call(
        scatter_kernel,
        out_shape=(
            jax.ShapeDtypeStruct(part, f32),
            jax.ShapeDtypeStruct(energy_part.shape, f32),
        ),
        in_specs=[pl.BlockSpec(memory_space=pltpu.VMEM)] * 2,
        out_specs=(pl.BlockSpec(memory_space=pltpu.VMEM),) * 2,
        scratch_shapes=[
            pltpu.VMEM((4, 2) + part, f32),
            pltpu.VMEM((4, 2) + part, f32),
            pltpu.VMEM((3,) + part, f32),
            pltpu.VMEM((3,) + part, f32),
            pltpu.VMEM((3,) + part, f32),
            pltpu.VMEM((3,) + part, f32),
            pltpu.VMEM((2,) + part, f32),
            pltpu.VMEM(part, f32),
            pltpu.VMEM((7,) + energy_part.shape, f32),
            pltpu.SemaphoreType.DMA((13,)),
            pltpu.SemaphoreType.DMA((13,)),
        ],
        compiler_params=pltpu.CompilerParams(
            collective_id=0, has_side_effects=True, vmem_limit_bytes=48 * 1024 * 1024
        ),
    )(grams, energy_part)


def smooth_rows(padded, stencil):
    pix_local = stencil.shape[1]
    total = jnp.zeros((padded.shape[0], pix_local), jnp.float32)
    for tap in range(5):
        total = total + stencil[tap][None, :] * padded[:, tap : tap + pix_local].astype(jnp.float32)
    return total.astype(jnp.bfloat16)


def row_squares(rows):
    values = rows.astype(jnp.float32)
    return jnp.sum(values * values, axis=1)


def on_device(images, stencil, pairs, live, rule_of_block, adduct):
    local_rows, pix_local = images.shape
    block = adduct.shape[1]
    local_blocks = local_rows // block
    shares = lax.axis_size("pix")
    rows = block // shares
    width = REACH * block
    ions = lax.axis_size("ion")
    up = [(i, i + 1) for i in range(ions - 1)]
    down = [(j, i) for i, j in up]
    raw_before = lax.ppermute(images[local_rows - width :], "ion", up)
    raw_after = lax.ppermute(images[:width], "ion", down)
    me_pix = lax.axis_index("pix")
    offset = me_pix * rows
    me_pix = lax.axis_index("pix")
    me_ion = lax.axis_index("ion")
    per_index = adduct.shape[0]
    half = per_index // 2
    by_ion = lax.all_gather(adduct[:half], "ion", axis=0, tiled=True)
    turn = [
        (p * ions + j, p * ions + (j - p) % ions)
        for j in range(ions)
        for p in range(1, shares)
    ]
    fetched = lax.ppermute(adduct[half:], ("pix", "ion"), turn)
    by_pix = lax.all_gather(jnp.where(me_pix == 0, adduct[half:], fetched), "pix", axis=0, tiled=True)
    lookup_tables = jnp.concatenate([by_ion, by_pix], axis=0)
    padded = extended_2(images, (("pix", 1),), 2)
    smoothed = smooth_rows(padded, stencil)
    local_squares = row_squares(smoothed)
    edges = jnp.concatenate([padded[:, :2], padded[:, pix_local + 2 :]], axis=1)
    edge_before = lax.ppermute(edges[local_rows - width :], "ion", up)
    edge_after = lax.ppermute(edges[:width], "ion", down)
    before = smooth_rows(
        jnp.concatenate([edge_before[:, :2], raw_before, edge_before[:, 2:]], axis=1), stencil
    )
    after = smooth_rows(
        jnp.concatenate([edge_after[:, :2], raw_after, edge_after[:, 2:]], axis=1), stencil
    )
    squares = jnp.concatenate([row_squares(before), local_squares, row_squares(after)])
    pixel_count = pix_local * shares
    first = lax.axis_index("ion") * local_blocks
    slots = pairs.shape[0]
    relative = pairs - first + REACH

    grams = pair_grams(relative, before, smoothed, after, shares, block)
    gram, energy_sum = scatter_grams(grams, squares.reshape(-1, block))
    inverse = 1.0 / jnp.sqrt(energy_sum.reshape(-1) / pixel_count + 1e-06)
    inv_blocks = inverse.reshape(local_blocks + 2 * REACH, block)

    inv_left = lax.dynamic_slice_in_dim(
        jnp.take(inv_blocks, relative[:, 0], axis=0), offset, rows, 1
    )
    inv_right = jnp.take(inv_blocks, relative[:, 1], axis=0)
    rules = jnp.take(rule_of_block, pairs[:, 1], axis=0)
    group, within = rules // per_index, rules % per_index
    rules = jnp.where(
        within < half,
        group * half + within,
        ions * half + ((group - me_ion) % ions) * half + within - half,
    )
    matrices = jnp.take(lookup_tables, rules, axis=0)
    coloc = (gram * inv_left[:, :, None] * inv_right[:, None, :] / pixel_count).astype(jnp.bfloat16)
    scores = jnp.einsum("src,scd->srd", coloc, matrices, preferred_element_type=jnp.float32)
    used = jnp.arange(slots, dtype=jnp.int32) < live[0]
    scores = jnp.where(used[:, None, None], scores, 0.0).astype(jnp.bfloat16)
    return (smoothed, scores)


def solution(mesh):
    return jax.shard_map(
        on_device,
        mesh=mesh,
        in_specs=(
            P("ion", "pix"),
            P(None, "pix"),
            P("ion", None),
            P("ion"),
            P(),
            P("ion", None, None),
        ),
        out_specs=(P("ion", "pix"), P("ion", "pix", None)),
        check_vma=False,
    )
```

```python
import jax
import jax.numpy as jnp
from jax import lax
from jax.experimental import pallas as pl
from jax.experimental.pallas import tpu as pltpu
from jax.sharding import PartitionSpec as P

REACH = 3


def extended_2(array, sides, width):
    for axis, dim in sides:
        size, length = (lax.axis_size(axis), array.shape[dim])
        up = [(i, (i + 1) % size) for i in range(size - 1)]
        down = [(j, i) for i, j in up]
        last = lax.slice_in_dim(array, length - width, length, axis=dim)
        first = lax.slice_in_dim(array, 0, width, axis=dim)
        before = lax.ppermute(last, axis, up)
        after = lax.ppermute(first, axis, down)
        array = jnp.concatenate([before, array, after], axis=dim)
    return array


def gram_kernel(shares, rel_ref, before_ref, local_ref, after_ref, chunk_ref, out_ref, table_out,
                ext_ref, table, sems, send_sems, recv_sems):
    block = out_ref.shape[-1]
    slots = out_ref.shape[-3]
    rows = out_ref.shape[-2]
    width = before_ref.shape[0]
    middle = local_ref.shape[0]
    p = lax.axis_index("pix")

    barrier = pltpu.get_barrier_semaphore()
    for k in range(1, shares):
        pl.semaphore_signal(barrier, 1, device_id={"pix": (p + k) % shares}, device_id_type=MESH)
    pl.semaphore_wait(barrier, shares - 1)
    sends = []
    for k in range(1, shares):
        dest = (p + k) % shares
        cp = pltpu.make_async_remote_copy(
            src_ref=chunk_ref, dst_ref=table.at[p], send_sem=send_sems.at[dest],
            recv_sem=recv_sems.at[p], device_id={"pix": dest}, device_id_type=MESH,
        )
        cp.start()
        sends.append(cp)

    copies = [
        pltpu.make_async_copy(local_ref, ext_ref.at[pl.ds(width, middle)], sems.at[0]),
        pltpu.make_async_copy(before_ref, ext_ref.at[pl.ds(0, width)], sems.at[1]),
        pltpu.make_async_copy(after_ref, ext_ref.at[pl.ds(width + middle, width)], sems.at[2]),
    ]
    for cp in copies:
        cp.start()
    for cp in copies:
        cp.wait()

    def body(s, carry):
        left = ext_ref[rel_ref[2 * s]]
        right = ext_ref[rel_ref[2 * s + 1]]
        g = lax.dot_general(
            left, right, (((1,), (1,)), ((), ())), preferred_element_type=jnp.float32
        )
        for q in range(shares):
            out_ref[q % 2, (q // 2) % 4, q // 8, s] = g[q * rows : (q + 1) * rows, :]
        return carry

    lax.fori_loop(0, slots, body, 0)

    for cp in sends:
        cp.wait_send()
    for k in range(1, shares):
        src = (p + shares - k) % shares
        pltpu.make_async_remote_copy(
            src_ref=chunk_ref, dst_ref=table.at[src], send_sem=send_sems.at[src],
            recv_sem=recv_sems.at[src], device_id={"pix": src}, device_id_type=MESH,
        ).wait_recv()
    table_out[p] = chunk_ref[...]
    for k in range(1, shares):
        src = (p + shares - k) % shares
        table_out[src] = table[src]


def pair_grams(relative, before, local, after, chunk, shares, block):
    slots = relative.shape[0]
    rows = block // shares
    pix_local = local.shape[1]
    ext_blocks = (before.shape[0] + local.shape[0] + after.shape[0]) // block
    ext_rows = ext_blocks * block
    flat = relative.reshape(-1).astype(jnp.int32)
    table_shape = (shares,) + chunk.shape
    before, local, after = (a.reshape(-1, block, pix_local) for a in (before, local, after))
    return pl.pallas_call(
        lambda *refs: gram_kernel(shares, *refs),
        out_shape=(
            jax.ShapeDtypeStruct((2, 4, 2, slots, rows, block), jnp.float32),
            jax.ShapeDtypeStruct(table_shape, chunk.dtype),
        ),
        in_specs=[pl.BlockSpec(memory_space=pltpu.SMEM)]
        + [pl.BlockSpec(memory_space=pl.ANY)] * 3
        + [pl.BlockSpec(memory_space=pltpu.VMEM)],
        out_specs=(pl.BlockSpec(memory_space=pltpu.VMEM),) * 2,
        scratch_shapes=[
            pltpu.VMEM((ext_blocks, block, pix_local), local.dtype),
            pltpu.VMEM(table_shape, chunk.dtype),
            pltpu.SemaphoreType.DMA((3,)),
            pltpu.SemaphoreType.DMA((shares,)),
            pltpu.SemaphoreType.DMA((shares,)),
        ],
        compiler_params=pltpu.CompilerParams(
            collective_id=1, has_side_effects=True, vmem_limit_bytes=56 * 1024 * 1024
        ),
        cost_estimate=pl.CostEstimate(
            flops=2 * slots * block * block * pix_local,
            transcendentals=0,
            bytes_accessed=ext_rows * pix_local * 2 + slots * block * block * 4,
        ),
    )(flat, before, local, after, chunk)

MESH = pl.DeviceIdType.MESH


def scatter_kernel(g_ref, e_ref, out_ref, eout_ref, r1, s1, recv_r, recv_l, acc_r, acc_l, tbuf, r3, ebuf, send_sem, recv_sem):
    p = lax.axis_index("pix")
    c = p % 2
    x = (p // 2) % 4
    yl = p // 8
    partner = p + 1 - 2 * c
    right = (yl * 4 + (x + 1) % 4) * 2 + c
    left = (yl * 4 + (x + 3) % 4) * 2 + c
    ypart = ((1 - yl) * 4 + x) * 2 + c

    barrier = pltpu.get_barrier_semaphore()
    for peer in (partner, right, left, ypart):
        pl.semaphore_signal(barrier, 1, device_id={"pix": peer}, device_id_type=MESH)
    pl.semaphore_wait(barrier, 4)

    def remote(src, dst, k, peer):
        return pltpu.make_async_remote_copy(
            src_ref=src, dst_ref=dst, send_sem=send_sem.at[k], recv_sem=recv_sem.at[k],
            device_id={"pix": peer}, device_id_type=MESH,
        )

    c1 = remote(g_ref.at[1 - c], r1, 0, partner)
    c1.start()
    ce1 = remote(e_ref, ebuf.at[0], 1, partner)
    ce1.start()
    c1.wait()
    ce1.wait()
    for j in range(4):
        s1[j] = g_ref[c, j] + r1[j]
    ebuf[1] = e_ref[...] + ebuf[0]

    done = []
    cr = cl = None
    for k in range(3):
        jr = (x + 3 - k) % 4
        jl = (x + k + 1) % 4
        if k == 0:
            src_r, src_l = s1.at[jr, 0], s1.at[jl, 1]
        else:
            cr.wait_recv()
            cl.wait_recv()
            acc_r[k] = s1[jr, 0] + recv_r[k - 1]
            acc_l[k] = s1[jl, 1] + recv_l[k - 1]
            src_r, src_l = acc_r.at[k], acc_l.at[k]
        cr = remote(src_r, recv_r.at[k], 2 + k, right)
        cr.start()
        cl = remote(src_l, recv_l.at[k], 5 + k, left)
        cl.start()
        done += [cr, cl]
        if k == 0:
            er = remote(ebuf.at[1], ebuf.at[2], 8, right)
            er.start()
            el = remote(ebuf.at[1], ebuf.at[3], 9, left)
            el.start()
            done += [er, el]
        if k == 1:
            er.wait_recv()
            ef = remote(ebuf.at[2], ebuf.at[4], 10, right)
            ef.start()
            done.append(ef)
    cr.wait_recv()
    cl.wait_recv()
    tbuf[0] = s1[x, 0] + recv_r[2]
    tbuf[1] = s1[x, 1] + recv_l[2]
    el.wait_recv()
    ef.wait_recv()
    ebuf[5] = ebuf[1] + ebuf[2] + ebuf[3] + ebuf[4]

    c3 = remote(tbuf.at[1 - yl], r3, 11, ypart)
    c3.start()
    ce3 = remote(ebuf.at[5], ebuf.at[6], 12, ypart)
    ce3.start()
    c3.wait()
    ce3.wait()
    out_ref[...] = tbuf[yl] + r3[...]
    eout_ref[...] = ebuf[5] + ebuf[6]
    for d in done:
        d.wait_send()


def scatter_grams(grams, energy_part):
    slots, rows, block = grams.shape[-3:]
    part = (slots, rows, block)
    f32 = jnp.float32
    return pl.pallas_call(
        scatter_kernel,
        out_shape=(
            jax.ShapeDtypeStruct(part, f32),
            jax.ShapeDtypeStruct(energy_part.shape, f32),
        ),
        in_specs=[pl.BlockSpec(memory_space=pltpu.VMEM)] * 2,
        out_specs=(pl.BlockSpec(memory_space=pltpu.VMEM),) * 2,
        scratch_shapes=[
            pltpu.VMEM((4, 2) + part, f32),
            pltpu.VMEM((4, 2) + part, f32),
            pltpu.VMEM((3,) + part, f32),
            pltpu.VMEM((3,) + part, f32),
            pltpu.VMEM((3,) + part, f32),
            pltpu.VMEM((3,) + part, f32),
            pltpu.VMEM((2,) + part, f32),
            pltpu.VMEM(part, f32),
            pltpu.VMEM((7,) + energy_part.shape, f32),
            pltpu.SemaphoreType.DMA((13,)),
            pltpu.SemaphoreType.DMA((13,)),
        ],
        compiler_params=pltpu.CompilerParams(
            collective_id=0, has_side_effects=True, vmem_limit_bytes=48 * 1024 * 1024
        ),
    )(grams, energy_part)


def smooth_rows(padded, stencil):
    pix_local = stencil.shape[1]
    total = jnp.zeros((padded.shape[0], pix_local), jnp.float32)
    for tap in range(5):
        total = total + stencil[tap][None, :] * padded[:, tap : tap + pix_local].astype(jnp.float32)
    return total.astype(jnp.bfloat16)


def row_squares(rows):
    values = rows.astype(jnp.float32)
    return jnp.sum(values * values, axis=1)


def on_device(images, stencil, pairs, live, rule_of_block, adduct):
    local_rows, pix_local = images.shape
    block = adduct.shape[1]
    local_blocks = local_rows // block
    shares = lax.axis_size("pix")
    rows = block // shares
    width = REACH * block
    ions = lax.axis_size("ion")
    up = [(i, i + 1) for i in range(ions - 1)]
    down = [(j, i) for i, j in up]
    raw_before = lax.ppermute(images[local_rows - width :], "ion", up)
    raw_after = lax.ppermute(images[:width], "ion", down)
    me_pix = lax.axis_index("pix")
    offset = me_pix * rows
    me_pix = lax.axis_index("pix")
    me_ion = lax.axis_index("ion")
    per_index = adduct.shape[0]
    turn = [
        (p * ions + j, p * ions + (j - p) % ions)
        for j in range(ions)
        for p in range(1, shares)
    ]
    fetched = lax.ppermute(adduct, ("pix", "ion"), turn)
    own_turn = jnp.where(me_pix == 0, adduct, fetched)
    padded = extended_2(images, (("pix", 1),), 2)
    smoothed = smooth_rows(padded, stencil)
    local_squares = row_squares(smoothed)
    edges = jnp.concatenate([padded[:, :2], padded[:, pix_local + 2 :]], axis=1)
    edge_before = lax.ppermute(edges[local_rows - width :], "ion", up)
    edge_after = lax.ppermute(edges[:width], "ion", down)
    before = smooth_rows(
        jnp.concatenate([edge_before[:, :2], raw_before, edge_before[:, 2:]], axis=1), stencil
    )
    after = smooth_rows(
        jnp.concatenate([edge_after[:, :2], raw_after, edge_after[:, 2:]], axis=1), stencil
    )
    squares = jnp.concatenate([row_squares(before), local_squares, row_squares(after)])
    pixel_count = pix_local * shares
    first = lax.axis_index("ion") * local_blocks
    slots = pairs.shape[0]
    relative = pairs - first + REACH

    grams, lookup_tables = pair_grams(relative, before, smoothed, after, own_turn, shares, block)
    lookup_tables = lookup_tables.reshape((-1,) + adduct.shape[1:])
    gram, energy_sum = scatter_grams(grams, squares.reshape(-1, block))
    inverse = 1.0 / jnp.sqrt(energy_sum.reshape(-1) / pixel_count + 1e-06)
    inv_blocks = inverse.reshape(local_blocks + 2 * REACH, block)

    inv_left = lax.dynamic_slice_in_dim(
        jnp.take(inv_blocks, relative[:, 0], axis=0), offset, rows, 1
    )
    inv_right = jnp.take(inv_blocks, relative[:, 1], axis=0)
    rules = jnp.take(rule_of_block, pairs[:, 1], axis=0)
    rules = ((rules // per_index - me_ion) % ions) * per_index + rules % per_index
    matrices = jnp.take(lookup_tables, rules, axis=0)
    coloc = (gram * inv_left[:, :, None] * inv_right[:, None, :] / pixel_count).astype(jnp.bfloat16)
    scores = jnp.einsum("src,scd->srd", coloc, matrices, preferred_element_type=jnp.float32)
    used = jnp.arange(slots, dtype=jnp.int32) < live[0]
    scores = jnp.where(used[:, None, None], scores, 0.0).astype(jnp.bfloat16)
    return (smoothed, scores)


def solution(mesh):
    return jax.shard_map(
        on_device,
        mesh=mesh,
        in_specs=(
            P("ion", "pix"),
            P(None, "pix"),
            P("ion", None),
            P("ion"),
            P(),
            P("ion", None, None),
        ),
        out_specs=(P("ion", "pix"), P("ion", "pix", None)),
        check_vma=False,
    )
```

```python
import jax
import jax.numpy as jnp
from jax import lax
from jax.experimental import pallas as pl
from jax.experimental.pallas import tpu as pltpu
from jax.sharding import PartitionSpec as P

REACH = 3


def extended_2(array, sides, width):
    for axis, dim in sides:
        size, length = (lax.axis_size(axis), array.shape[dim])
        up = [(i, (i + 1) % size) for i in range(size - 1)]
        down = [(j, i) for i, j in up]
        last = lax.slice_in_dim(array, length - width, length, axis=dim)
        first = lax.slice_in_dim(array, 0, width, axis=dim)
        before = lax.ppermute(last, axis, up)
        after = lax.ppermute(first, axis, down)
        array = jnp.concatenate([before, array, after], axis=dim)
    return array


def gram_kernel(shares, rel_ref, before_ref, local_ref, after_ref, chunk_ref, out_ref, table_out,
                ext_ref, table, sems, send_sems, recv_sems):
    block = out_ref.shape[-1]
    slots = out_ref.shape[-3]
    rows = out_ref.shape[-2]
    width = before_ref.shape[0]
    middle = local_ref.shape[0]
    p = lax.axis_index("pix")
    c = p % 2
    x = (p // 2) % 4
    yl = p // 8
    partner = p + 1 - 2 * c
    right = (yl * 4 + (x + 1) % 4) * 2 + c
    left = (yl * 4 + (x + 3) % 4) * 2 + c
    ypart = ((1 - yl) * 4 + x) * 2 + c
    mine = c * 8 + x * 2 + yl
    theirs = c * 8 + x * 2 + 1 - yl
    pair_at = c * 8 + x * 2
    from_left = c * 8 + ((x + 3) % 4) * 2

    barrier = pltpu.get_barrier_semaphore()
    for peer in (partner, right, left, ypart):
        pl.semaphore_signal(barrier, 1, device_id={"pix": peer}, device_id_type=MESH)
    pl.semaphore_wait(barrier, 4)

    def remote(src, dst, k, peer):
        return pltpu.make_async_remote_copy(
            src_ref=src, dst_ref=dst, send_sem=send_sems.at[k], recv_sem=recv_sems.at[k],
            device_id={"pix": peer}, device_id_type=MESH,
        )

    sent = []
    ca = remote(chunk_ref, table.at[mine], 0, ypart)
    ca.start()
    sent.append(ca)
    own = pltpu.make_async_copy(chunk_ref, table.at[mine], sems.at[3])
    own.start()

    copies = [
        pltpu.make_async_copy(local_ref, ext_ref.at[pl.ds(width, middle)], sems.at[0]),
        pltpu.make_async_copy(before_ref, ext_ref.at[pl.ds(0, width)], sems.at[1]),
        pltpu.make_async_copy(after_ref, ext_ref.at[pl.ds(width + middle, width)], sems.at[2]),
    ]
    for cp in copies:
        cp.start()
    for cp in copies:
        cp.wait()

    def body(s, carry):
        left_rows = ext_ref[rel_ref[2 * s]]
        right_rows = ext_ref[rel_ref[2 * s + 1]]
        g = lax.dot_general(
            left_rows, right_rows, (((1,), (1,)), ((), ())), preferred_element_type=jnp.float32
        )
        for q in range(shares):
            out_ref[q % 2, (q // 2) % 4, q // 8, s] = g[q * rows : (q + 1) * rows, :]
        return carry

    third = slots // 3
    lax.fori_loop(0, third, body, 0)
    ca.wait_recv()
    b1 = [
        remote(chunk_ref, table.at[mine], 1, right),
        remote(table.at[theirs], table.at[theirs], 2, right),
        remote(chunk_ref, table.at[mine], 3, left),
        remote(table.at[theirs], table.at[theirs], 4, left),
    ]
    for cp in b1:
        cp.start()
    sent += b1
    lax.fori_loop(third, 2 * third, body, 0)
    for cp in b1:
        cp.wait_recv()
    b2 = remote(table.at[pl.ds(from_left, 2)], table.at[pl.ds(from_left, 2)], 5, right)
    b2.start()
    sent.append(b2)
    lax.fori_loop(2 * third, slots, body, 0)
    b2.wait_recv()
    own.wait()
    cc = remote(table.at[pl.ds(c * 8, 8)], table.at[pl.ds(c * 8, 8)], 6, partner)
    cc.start()
    sent.append(cc)
    cc.wait_recv()
    for cp in sent:
        cp.wait_send()
    table_out[...] = table[...]


def pair_grams(relative, before, local, after, chunk, shares, block):
    slots = relative.shape[0]
    rows = block // shares
    pix_local = local.shape[1]
    ext_blocks = (before.shape[0] + local.shape[0] + after.shape[0]) // block
    ext_rows = ext_blocks * block
    flat = relative.reshape(-1).astype(jnp.int32)
    table_shape = (shares,) + chunk.shape
    before, local, after = (a.reshape(-1, block, pix_local) for a in (before, local, after))
    return pl.pallas_call(
        lambda *refs: gram_kernel(shares, *refs),
        out_shape=(
            jax.ShapeDtypeStruct((2, 4, 2, slots, rows, block), jnp.float32),
            jax.ShapeDtypeStruct(table_shape, chunk.dtype),
        ),
        in_specs=[pl.BlockSpec(memory_space=pltpu.SMEM)]
        + [pl.BlockSpec(memory_space=pl.ANY)] * 3
        + [pl.BlockSpec(memory_space=pltpu.VMEM)],
        out_specs=(pl.BlockSpec(memory_space=pltpu.VMEM),) * 2,
        scratch_shapes=[
            pltpu.VMEM((ext_blocks, block, pix_local), local.dtype),
            pltpu.VMEM(table_shape, chunk.dtype),
            pltpu.SemaphoreType.DMA((4,)),
            pltpu.SemaphoreType.DMA((7,)),
            pltpu.SemaphoreType.DMA((7,)),
        ],
        compiler_params=pltpu.CompilerParams(
            collective_id=1, has_side_effects=True, vmem_limit_bytes=56 * 1024 * 1024
        ),
        cost_estimate=pl.CostEstimate(
            flops=2 * slots * block * block * pix_local,
            transcendentals=0,
            bytes_accessed=ext_rows * pix_local * 2 + slots * block * block * 4,
        ),
    )(flat, before, local, after, chunk)

MESH = pl.DeviceIdType.MESH


def scatter_kernel(g_ref, e_ref, out_ref, eout_ref, r1, s1, recv_r, recv_l, acc_r, acc_l, tbuf, r3, ebuf, send_sem, recv_sem):
    p = lax.axis_index("pix")
    c = p % 2
    x = (p // 2) % 4
    yl = p // 8
    partner = p + 1 - 2 * c
    right = (yl * 4 + (x + 1) % 4) * 2 + c
    left = (yl * 4 + (x + 3) % 4) * 2 + c
    ypart = ((1 - yl) * 4 + x) * 2 + c

    barrier = pltpu.get_barrier_semaphore()
    for peer in (partner, right, left, ypart):
        pl.semaphore_signal(barrier, 1, device_id={"pix": peer}, device_id_type=MESH)
    pl.semaphore_wait(barrier, 4)

    def remote(src, dst, k, peer):
        return pltpu.make_async_remote_copy(
            src_ref=src, dst_ref=dst, send_sem=send_sem.at[k], recv_sem=recv_sem.at[k],
            device_id={"pix": peer}, device_id_type=MESH,
        )

    c1 = remote(g_ref.at[1 - c], r1, 0, partner)
    c1.start()
    ce1 = remote(e_ref, ebuf.at[0], 1, partner)
    ce1.start()
    c1.wait()
    ce1.wait()
    for j in range(4):
        s1[j] = g_ref[c, j] + r1[j]
    ebuf[1] = e_ref[...] + ebuf[0]

    done = []
    cr = cl = None
    for k in range(3):
        jr = (x + 3 - k) % 4
        jl = (x + k + 1) % 4
        if k == 0:
            src_r, src_l = s1.at[jr, 0], s1.at[jl, 1]
        else:
            cr.wait_recv()
            cl.wait_recv()
            acc_r[k] = s1[jr, 0] + recv_r[k - 1]
            acc_l[k] = s1[jl, 1] + recv_l[k - 1]
            src_r, src_l = acc_r.at[k], acc_l.at[k]
        cr = remote(src_r, recv_r.at[k], 2 + k, right)
        cr.start()
        cl = remote(src_l, recv_l.at[k], 5 + k, left)
        cl.start()
        done += [cr, cl]
        if k == 0:
            er = remote(ebuf.at[1], ebuf.at[2], 8, right)
            er.start()
            el = remote(ebuf.at[1], ebuf.at[3], 9, left)
            el.start()
            done += [er, el]
        if k == 1:
            er.wait_recv()
            ef = remote(ebuf.at[2], ebuf.at[4], 10, right)
            ef.start()
            done.append(ef)
    cr.wait_recv()
    cl.wait_recv()
    tbuf[0] = s1[x, 0] + recv_r[2]
    tbuf[1] = s1[x, 1] + recv_l[2]
    el.wait_recv()
    ef.wait_recv()
    ebuf[5] = ebuf[1] + ebuf[2] + ebuf[3] + ebuf[4]

    c3 = remote(tbuf.at[1 - yl], r3, 11, ypart)
    c3.start()
    ce3 = remote(ebuf.at[5], ebuf.at[6], 12, ypart)
    ce3.start()
    c3.wait()
    ce3.wait()
    out_ref[...] = tbuf[yl] + r3[...]
    eout_ref[...] = ebuf[5] + ebuf[6]
    for d in done:
        d.wait_send()


def scatter_grams(grams, energy_part):
    slots, rows, block = grams.shape[-3:]
    part = (slots, rows, block)
    f32 = jnp.float32
    return pl.pallas_call(
        scatter_kernel,
        out_shape=(
            jax.ShapeDtypeStruct(part, f32),
            jax.ShapeDtypeStruct(energy_part.shape, f32),
        ),
        in_specs=[pl.BlockSpec(memory_space=pltpu.VMEM)] * 2,
        out_specs=(pl.BlockSpec(memory_space=pltpu.VMEM),) * 2,
        scratch_shapes=[
            pltpu.VMEM((4, 2) + part, f32),
            pltpu.VMEM((4, 2) + part, f32),
            pltpu.VMEM((3,) + part, f32),
            pltpu.VMEM((3,) + part, f32),
            pltpu.VMEM((3,) + part, f32),
            pltpu.VMEM((3,) + part, f32),
            pltpu.VMEM((2,) + part, f32),
            pltpu.VMEM(part, f32),
            pltpu.VMEM((7,) + energy_part.shape, f32),
            pltpu.SemaphoreType.DMA((13,)),
            pltpu.SemaphoreType.DMA((13,)),
        ],
        compiler_params=pltpu.CompilerParams(
            collective_id=0, has_side_effects=True, vmem_limit_bytes=48 * 1024 * 1024
        ),
    )(grams, energy_part)


def smooth_rows(padded, stencil):
    pix_local = stencil.shape[1]
    total = jnp.zeros((padded.shape[0], pix_local), jnp.float32)
    for tap in range(5):
        total = total + stencil[tap][None, :] * padded[:, tap : tap + pix_local].astype(jnp.float32)
    return total.astype(jnp.bfloat16)


def row_squares(rows):
    values = rows.astype(jnp.float32)
    return jnp.sum(values * values, axis=1)


def on_device(images, stencil, pairs, live, rule_of_block, adduct):
    local_rows, pix_local = images.shape
    block = adduct.shape[1]
    local_blocks = local_rows // block
    shares = lax.axis_size("pix")
    rows = block // shares
    width = REACH * block
    ions = lax.axis_size("ion")
    up = [(i, i + 1) for i in range(ions - 1)]
    down = [(j, i) for i, j in up]
    raw_before = lax.ppermute(images[local_rows - width :], "ion", up)
    raw_after = lax.ppermute(images[:width], "ion", down)
    me_pix = lax.axis_index("pix")
    offset = me_pix * rows
    me_pix = lax.axis_index("pix")
    me_ion = lax.axis_index("ion")
    per_index = adduct.shape[0]
    turn = [
        (p * ions + j, p * ions + (j - p) % ions)
        for j in range(ions)
        for p in range(1, shares)
    ]
    fetched = lax.ppermute(adduct, ("pix", "ion"), turn)
    own_turn = jnp.where(me_pix == 0, adduct, fetched)
    padded = extended_2(images, (("pix", 1),), 2)
    smoothed = smooth_rows(padded, stencil)
    local_squares = row_squares(smoothed)
    edges = jnp.concatenate([padded[:, :2], padded[:, pix_local + 2 :]], axis=1)
    edge_before = lax.ppermute(edges[local_rows - width :], "ion", up)
    edge_after = lax.ppermute(edges[:width], "ion", down)
    before = smooth_rows(
        jnp.concatenate([edge_before[:, :2], raw_before, edge_before[:, 2:]], axis=1), stencil
    )
    after = smooth_rows(
        jnp.concatenate([edge_after[:, :2], raw_after, edge_after[:, 2:]], axis=1), stencil
    )
    squares = jnp.concatenate([row_squares(before), local_squares, row_squares(after)])
    pixel_count = pix_local * shares
    first = lax.axis_index("ion") * local_blocks
    slots = pairs.shape[0]
    relative = pairs - first + REACH

    grams, lookup_tables = pair_grams(relative, before, smoothed, after, own_turn, shares, block)
    lookup_tables = lookup_tables.reshape((-1,) + adduct.shape[1:])
    gram, energy_sum = scatter_grams(grams, squares.reshape(-1, block))
    inverse = 1.0 / jnp.sqrt(energy_sum.reshape(-1) / pixel_count + 1e-06)
    inv_blocks = inverse.reshape(local_blocks + 2 * REACH, block)

    inv_left = lax.dynamic_slice_in_dim(
        jnp.take(inv_blocks, relative[:, 0], axis=0), offset, rows, 1
    )
    inv_right = jnp.take(inv_blocks, relative[:, 1], axis=0)
    rules = jnp.take(rule_of_block, pairs[:, 1], axis=0)
    source = (rules // per_index - me_ion) % ions
    slot = (source % 2) * 8 + ((source // 2) % 4) * 2 + source // 8
    rules = slot * per_index + rules % per_index
    matrices = jnp.take(lookup_tables, rules, axis=0)
    coloc = (gram * inv_left[:, :, None] * inv_right[:, None, :] / pixel_count).astype(jnp.bfloat16)
    scores = jnp.einsum("src,scd->srd", coloc, matrices, preferred_element_type=jnp.float32)
    used = jnp.arange(slots, dtype=jnp.int32) < live[0]
    scores = jnp.where(used[:, None, None], scores, 0.0).astype(jnp.bfloat16)
    return (smoothed, scores)


def solution(mesh):
    return jax.shard_map(
        on_device,
        mesh=mesh,
        in_specs=(
            P("ion", "pix"),
            P(None, "pix"),
            P("ion", None),
            P("ion"),
            P(),
            P("ion", None, None),
        ),
        out_specs=(P("ion", "pix"), P("ion", "pix", None)),
        check_vma=False,
    )
```

```python
import jax
import jax.numpy as jnp
from jax import lax
from jax.experimental import pallas as pl
from jax.experimental.pallas import tpu as pltpu
from jax.sharding import PartitionSpec as P

REACH = 3


def extended_2(array, sides, width):
    for axis, dim in sides:
        size, length = (lax.axis_size(axis), array.shape[dim])
        up = [(i, (i + 1) % size) for i in range(size - 1)]
        down = [(j, i) for i, j in up]
        last = lax.slice_in_dim(array, length - width, length, axis=dim)
        first = lax.slice_in_dim(array, 0, width, axis=dim)
        before = lax.ppermute(last, axis, up)
        after = lax.ppermute(first, axis, down)
        array = jnp.concatenate([before, array, after], axis=dim)
    return array


def gram_kernel(shares, rel_ref, before_ref, local_ref, after_ref, chunk_ref, out_ref, table_out,
                ext_ref, table, sems, send_sems, recv_sems):
    block = out_ref.shape[-1]
    slots = out_ref.shape[-3]
    rows = out_ref.shape[-2]
    width = before_ref.shape[0]
    middle = local_ref.shape[0]
    p = lax.axis_index("pix")
    c = p % 2
    x = (p // 2) % 4
    yl = p // 8
    partner = p + 1 - 2 * c
    right = (yl * 4 + (x + 1) % 4) * 2 + c
    left = (yl * 4 + (x + 3) % 4) * 2 + c
    ypart = ((1 - yl) * 4 + x) * 2 + c
    mine = c * 8 + x * 2 + yl
    theirs = c * 8 + x * 2 + 1 - yl
    pair_at = c * 8 + x * 2
    from_left = c * 8 + ((x + 3) % 4) * 2

    barrier = pltpu.get_barrier_semaphore()
    for peer in (partner, right, left, ypart):
        pl.semaphore_signal(barrier, 1, device_id={"pix": peer}, device_id_type=MESH)
    pl.semaphore_wait(barrier, 4)

    def remote(src, dst, k, peer):
        return pltpu.make_async_remote_copy(
            src_ref=src, dst_ref=dst, send_sem=send_sems.at[k], recv_sem=recv_sems.at[k],
            device_id={"pix": peer}, device_id_type=MESH,
        )

    sent = []
    ca = remote(chunk_ref, table.at[mine], 0, ypart)
    ca.start()
    sent.append(ca)
    own = pltpu.make_async_copy(chunk_ref, table.at[mine], sems.at[3])
    own.start()

    copies = [
        pltpu.make_async_copy(local_ref, ext_ref.at[pl.ds(width, middle)], sems.at[0]),
        pltpu.make_async_copy(before_ref, ext_ref.at[pl.ds(0, width)], sems.at[1]),
        pltpu.make_async_copy(after_ref, ext_ref.at[pl.ds(width + middle, width)], sems.at[2]),
    ]
    for cp in copies:
        cp.start()
    for cp in copies:
        cp.wait()

    def body(s, carry):
        left_rows = ext_ref[rel_ref[2 * s]]
        right_rows = ext_ref[rel_ref[2 * s + 1]]
        g = lax.dot_general(
            left_rows, right_rows, (((1,), (1,)), ((), ())), preferred_element_type=jnp.float32
        )
        for q in range(shares):
            out_ref[q % 2, (q // 2) % 4, q // 8, s] = g[q * rows : (q + 1) * rows, :]
        return carry

    third = slots // 3
    lax.fori_loop(0, third, body, 0)
    ca.wait_recv()
    b1 = [
        remote(chunk_ref, table.at[mine], 1, right),
        remote(table.at[theirs], table.at[theirs], 2, right),
        remote(chunk_ref, table.at[mine], 3, left),
        remote(table.at[theirs], table.at[theirs], 4, left),
    ]
    for cp in b1:
        cp.start()
    sent += b1
    lax.fori_loop(third, 2 * third, body, 0)
    for cp in b1:
        cp.wait_recv()
    b2 = remote(table.at[pl.ds(from_left, 2)], table.at[pl.ds(from_left, 2)], 5, right)
    b2.start()
    sent.append(b2)
    lax.fori_loop(2 * third, slots, body, 0)
    b2.wait_recv()
    own.wait()
    cc = remote(table.at[pl.ds(c * 8, 8)], table.at[pl.ds(c * 8, 8)], 6, partner)
    cc.start()
    sent.append(cc)
    cc.wait_recv()
    for cp in sent:
        cp.wait_send()
    table_out[...] = table[...]


def pair_grams(relative, before, local, after, chunk, shares, block):
    slots = relative.shape[0]
    rows = block // shares
    pix_local = local.shape[1]
    ext_blocks = (before.shape[0] + local.shape[0] + after.shape[0]) // block
    ext_rows = ext_blocks * block
    flat = relative.reshape(-1).astype(jnp.int32)
    table_shape = (shares,) + chunk.shape
    before, local, after = (a.reshape(-1, block, pix_local) for a in (before, local, after))
    return pl.pallas_call(
        lambda *refs: gram_kernel(shares, *refs),
        out_shape=(
            jax.ShapeDtypeStruct((2, 4, 2, slots, rows, block), jnp.float32),
            jax.ShapeDtypeStruct(table_shape, chunk.dtype),
        ),
        in_specs=[pl.BlockSpec(memory_space=pltpu.SMEM)]
        + [pl.BlockSpec(memory_space=pl.ANY)] * 3
        + [pl.BlockSpec(memory_space=pltpu.VMEM)],
        out_specs=(pl.BlockSpec(memory_space=pltpu.VMEM),) * 2,
        scratch_shapes=[
            pltpu.VMEM((ext_blocks, block, pix_local), local.dtype),
            pltpu.VMEM(table_shape, chunk.dtype),
            pltpu.SemaphoreType.DMA((4,)),
            pltpu.SemaphoreType.DMA((7,)),
            pltpu.SemaphoreType.DMA((7,)),
        ],
        compiler_params=pltpu.CompilerParams(
            collective_id=1, has_side_effects=True, vmem_limit_bytes=56 * 1024 * 1024
        ),
        cost_estimate=pl.CostEstimate(
            flops=2 * slots * block * block * pix_local,
            transcendentals=0,
            bytes_accessed=ext_rows * pix_local * 2 + slots * block * block * 4,
        ),
    )(flat, before, local, after, chunk)

MESH = pl.DeviceIdType.MESH


def scatter_kernel(g_ref, e_ref, out_ref, eout_ref, r1, s1, recv_r, recv_l, acc_r, acc_l, tbuf, r3, ebuf, send_sem, recv_sem):
    p = lax.axis_index("pix")
    c = p % 2
    x = (p // 2) % 4
    yl = p // 8
    partner = p + 1 - 2 * c
    right = (yl * 4 + (x + 1) % 4) * 2 + c
    left = (yl * 4 + (x + 3) % 4) * 2 + c
    ypart = ((1 - yl) * 4 + x) * 2 + c

    barrier = pltpu.get_barrier_semaphore()
    for peer in (partner, right, left, ypart):
        pl.semaphore_signal(barrier, 1, device_id={"pix": peer}, device_id_type=MESH)
    pl.semaphore_wait(barrier, 4)

    def remote(src, dst, k, peer):
        return pltpu.make_async_remote_copy(
            src_ref=src, dst_ref=dst, send_sem=send_sem.at[k], recv_sem=recv_sem.at[k],
            device_id={"pix": peer}, device_id_type=MESH,
        )

    c1 = remote(g_ref.at[1 - c], r1, 0, partner)
    c1.start()
    ce1 = remote(e_ref, ebuf.at[0], 1, partner)
    ce1.start()
    c1.wait()
    ce1.wait()
    for j in range(4):
        s1[j] = g_ref[c, j] + r1[j]
    ebuf[1] = e_ref[...] + ebuf[0]

    done = []
    cr = cl = None
    for k in range(3):
        jr = (x + 3 - k) % 4
        jl = (x + k + 1) % 4
        if k == 0:
            src_r, src_l = s1.at[jr, 0], s1.at[jl, 1]
        else:
            cr.wait_recv()
            cl.wait_recv()
            acc_r[k] = s1[jr, 0] + recv_r[k - 1]
            acc_l[k] = s1[jl, 1] + recv_l[k - 1]
            src_r, src_l = acc_r.at[k], acc_l.at[k]
        cr = remote(src_r, recv_r.at[k], 2 + k, right)
        cr.start()
        cl = remote(src_l, recv_l.at[k], 5 + k, left)
        cl.start()
        done += [cr, cl]
        if k == 0:
            er = remote(ebuf.at[1], ebuf.at[2], 8, right)
            er.start()
            el = remote(ebuf.at[1], ebuf.at[3], 9, left)
            el.start()
            done += [er, el]
        if k == 1:
            er.wait_recv()
            ef = remote(ebuf.at[2], ebuf.at[4], 10, right)
            ef.start()
            done.append(ef)
    cr.wait_recv()
    cl.wait_recv()
    tbuf[0] = s1[x, 0] + recv_r[2]
    tbuf[1] = s1[x, 1] + recv_l[2]
    el.wait_recv()
    ef.wait_recv()
    ebuf[5] = ebuf[1] + ebuf[2] + ebuf[3] + ebuf[4]

    c3 = remote(tbuf.at[1 - yl], r3, 11, ypart)
    c3.start()
    ce3 = remote(ebuf.at[5], ebuf.at[6], 12, ypart)
    ce3.start()
    c3.wait()
    ce3.wait()
    out_ref[...] = tbuf[yl] + r3[...]
    eout_ref[...] = ebuf[5] + ebuf[6]
    for d in done:
        d.wait_send()


def scatter_grams(grams, energy_part):
    slots, rows, block = grams.shape[-3:]
    part = (slots, rows, block)
    f32 = jnp.float32
    return pl.pallas_call(
        scatter_kernel,
        out_shape=(
            jax.ShapeDtypeStruct(part, f32),
            jax.ShapeDtypeStruct(energy_part.shape, f32),
        ),
        in_specs=[pl.BlockSpec(memory_space=pltpu.VMEM)] * 2,
        out_specs=(pl.BlockSpec(memory_space=pltpu.VMEM),) * 2,
        scratch_shapes=[
            pltpu.VMEM((4, 2) + part, f32),
            pltpu.VMEM((4, 2) + part, f32),
            pltpu.VMEM((3,) + part, f32),
            pltpu.VMEM((3,) + part, f32),
            pltpu.VMEM((3,) + part, f32),
            pltpu.VMEM((3,) + part, f32),
            pltpu.VMEM((2,) + part, f32),
            pltpu.VMEM(part, f32),
            pltpu.VMEM((7,) + energy_part.shape, f32),
            pltpu.SemaphoreType.DMA((13,)),
            pltpu.SemaphoreType.DMA((13,)),
        ],
        compiler_params=pltpu.CompilerParams(
            collective_id=0, has_side_effects=True, vmem_limit_bytes=48 * 1024 * 1024
        ),
    )(grams, energy_part)


def smooth_rows(padded, stencil):
    pix_local = stencil.shape[1]
    total = jnp.zeros((padded.shape[0], pix_local), jnp.float32)
    for tap in range(5):
        total = total + stencil[tap][None, :] * padded[:, tap : tap + pix_local].astype(jnp.float32)
    return total.astype(jnp.bfloat16)


def row_squares(rows):
    values = rows.astype(jnp.float32)
    return jnp.sum(values * values, axis=1)


def on_device(images, stencil, pairs, live, rule_of_block, adduct):
    local_rows, pix_local = images.shape
    block = adduct.shape[1]
    local_blocks = local_rows // block
    shares = lax.axis_size("pix")
    rows = block // shares
    width = REACH * block
    ions = lax.axis_size("ion")
    up = [(i, i + 1) for i in range(ions - 1)]
    down = [(j, i) for i, j in up]
    me_pix = lax.axis_index("pix")
    offset = me_pix * rows
    me_pix = lax.axis_index("pix")
    me_ion = lax.axis_index("ion")
    per_index = adduct.shape[0]
    turn = [
        (p * ions + j, p * ions + (j - p) % ions)
        for j in range(ions)
        for p in range(1, shares)
    ]
    fetched = lax.ppermute(adduct, ("pix", "ion"), turn)
    own_turn = jnp.where(me_pix == 0, adduct, fetched)
    padded = extended_2(images, (("pix", 1),), 2)
    raw_before = lax.ppermute(padded[local_rows - width :], "ion", up)
    raw_after = lax.ppermute(padded[:width], "ion", down)
    smoothed = smooth_rows(padded, stencil)
    local_squares = row_squares(smoothed)
    before = smooth_rows(raw_before, stencil)
    after = smooth_rows(raw_after, stencil)
    squares = jnp.concatenate([row_squares(before), local_squares, row_squares(after)])
    pixel_count = pix_local * shares
    first = lax.axis_index("ion") * local_blocks
    slots = pairs.shape[0]
    relative = pairs - first + REACH

    grams, lookup_tables = pair_grams(relative, before, smoothed, after, own_turn, shares, block)
    lookup_tables = lookup_tables.reshape((-1,) + adduct.shape[1:])
    gram, energy_sum = scatter_grams(grams, squares.reshape(-1, block))
    inverse = 1.0 / jnp.sqrt(energy_sum.reshape(-1) / pixel_count + 1e-06)
    inv_blocks = inverse.reshape(local_blocks + 2 * REACH, block)

    inv_left = lax.dynamic_slice_in_dim(
        jnp.take(inv_blocks, relative[:, 0], axis=0), offset, rows, 1
    )
    inv_right = jnp.take(inv_blocks, relative[:, 1], axis=0)
    rules = jnp.take(rule_of_block, pairs[:, 1], axis=0)
    source = (rules // per_index - me_ion) % ions
    slot = (source % 2) * 8 + ((source // 2) % 4) * 2 + source // 8
    rules = slot * per_index + rules % per_index
    matrices = jnp.take(lookup_tables, rules, axis=0)
    coloc = (gram * inv_left[:, :, None] * inv_right[:, None, :] / pixel_count).astype(jnp.bfloat16)
    scores = jnp.einsum("src,scd->srd", coloc, matrices, preferred_element_type=jnp.float32)
    used = jnp.arange(slots, dtype=jnp.int32) < live[0]
    scores = jnp.where(used[:, None, None], scores, 0.0).astype(jnp.bfloat16)
    return (smoothed, scores)


def solution(mesh):
    return jax.shard_map(
        on_device,
        mesh=mesh,
        in_specs=(
            P("ion", "pix"),
            P(None, "pix"),
            P("ion", None),
            P("ion"),
            P(),
            P("ion", None, None),
        ),
        out_specs=(P("ion", "pix"), P("ion", "pix", None)),
        check_vma=False,
    )
```

```python
import jax
import jax.numpy as jnp
from jax import lax
from jax.experimental import pallas as pl
from jax.experimental.pallas import tpu as pltpu
from jax.sharding import PartitionSpec as P

REACH = 3


def extended_2(array, sides, width):
    for axis, dim in sides:
        size, length = (lax.axis_size(axis), array.shape[dim])
        up = [(i, (i + 1) % size) for i in range(size - 1)]
        down = [(j, i) for i, j in up]
        last = lax.slice_in_dim(array, length - width, length, axis=dim)
        first = lax.slice_in_dim(array, 0, width, axis=dim)
        before = lax.ppermute(last, axis, up)
        after = lax.ppermute(first, axis, down)
        array = jnp.concatenate([before, array, after], axis=dim)
    return array


def gram_kernel(shares, rel_ref, before_ref, local_ref, after_ref, chunk_ref, out_ref, table_out,
                ext_ref, table, sems, send_sems, recv_sems):
    block = out_ref.shape[-1]
    slots = out_ref.shape[-3]
    rows = out_ref.shape[-2]
    width = before_ref.shape[0]
    middle = local_ref.shape[0]
    p = lax.axis_index("pix")
    c = p % 2
    x = (p // 2) % 4
    yl = p // 8
    partner = p + 1 - 2 * c
    right = (yl * 4 + (x + 1) % 4) * 2 + c
    left = (yl * 4 + (x + 3) % 4) * 2 + c
    ypart = ((1 - yl) * 4 + x) * 2 + c
    mine = c * 8 + x * 2 + yl
    theirs = c * 8 + x * 2 + 1 - yl
    pair_at = c * 8 + x * 2
    from_left = c * 8 + ((x + 3) % 4) * 2

    barrier = pltpu.get_barrier_semaphore()
    for peer in (partner, right, left, ypart):
        pl.semaphore_signal(barrier, 1, device_id={"pix": peer}, device_id_type=MESH)
    pl.semaphore_wait(barrier, 4)

    def remote(src, dst, k, peer):
        return pltpu.make_async_remote_copy(
            src_ref=src, dst_ref=dst, send_sem=send_sems.at[k], recv_sem=recv_sems.at[k],
            device_id={"pix": peer}, device_id_type=MESH,
        )

    sent = []
    ca = remote(chunk_ref, table.at[mine], 0, ypart)
    ca.start()
    sent.append(ca)
    own = pltpu.make_async_copy(chunk_ref, table.at[mine], sems.at[3])
    own.start()

    copies = [
        pltpu.make_async_copy(local_ref, ext_ref.at[pl.ds(width, middle)], sems.at[0]),
        pltpu.make_async_copy(before_ref, ext_ref.at[pl.ds(0, width)], sems.at[1]),
        pltpu.make_async_copy(after_ref, ext_ref.at[pl.ds(width + middle, width)], sems.at[2]),
    ]
    for cp in copies:
        cp.start()
    for cp in copies:
        cp.wait()

    def body(s, carry):
        left_rows = ext_ref[rel_ref[2 * s]]
        right_rows = ext_ref[rel_ref[2 * s + 1]]
        g = lax.dot_general(
            left_rows, right_rows, (((1,), (1,)), ((), ())), preferred_element_type=jnp.float32
        )
        for q in range(shares):
            out_ref[q % 2, (q // 2) % 4, q // 8, s] = g[q * rows : (q + 1) * rows, :]
        return carry

    third = slots // 3
    lax.fori_loop(0, third, body, 0)
    ca.wait_recv()
    b1 = [
        remote(chunk_ref, table.at[mine], 1, right),
        remote(table.at[theirs], table.at[theirs], 2, right),
        remote(chunk_ref, table.at[mine], 3, left),
        remote(table.at[theirs], table.at[theirs], 4, left),
    ]
    for cp in b1:
        cp.start()
    sent += b1
    lax.fori_loop(third, 2 * third, body, 0)
    for cp in b1:
        cp.wait_recv()
    b2 = remote(table.at[pl.ds(from_left, 2)], table.at[pl.ds(from_left, 2)], 5, right)
    b2.start()
    sent.append(b2)
    lax.fori_loop(2 * third, slots, body, 0)
    b2.wait_recv()
    own.wait()
    cc = remote(table.at[pl.ds(c * 8, 8)], table.at[pl.ds(c * 8, 8)], 6, partner)
    cc.start()
    sent.append(cc)
    cc.wait_recv()
    for cp in sent:
        cp.wait_send()
    table_out[...] = table[...]


def pair_grams(relative, before, local, after, chunk, shares, block):
    slots = relative.shape[0]
    rows = block // shares
    pix_local = local.shape[1]
    ext_blocks = (before.shape[0] + local.shape[0] + after.shape[0]) // block
    ext_rows = ext_blocks * block
    flat = relative.reshape(-1).astype(jnp.int32)
    table_shape = (shares,) + chunk.shape
    before, local, after = (a.reshape(-1, block, pix_local) for a in (before, local, after))
    return pl.pallas_call(
        lambda *refs: gram_kernel(shares, *refs),
        out_shape=(
            jax.ShapeDtypeStruct((2, 4, 2, slots, rows, block), jnp.float32),
            jax.ShapeDtypeStruct(table_shape, chunk.dtype),
        ),
        in_specs=[pl.BlockSpec(memory_space=pltpu.SMEM)]
        + [pl.BlockSpec(memory_space=pl.ANY)] * 3
        + [pl.BlockSpec(memory_space=pltpu.VMEM)],
        out_specs=(pl.BlockSpec(memory_space=pltpu.VMEM),) * 2,
        scratch_shapes=[
            pltpu.VMEM((ext_blocks, block, pix_local), local.dtype),
            pltpu.VMEM(table_shape, chunk.dtype),
            pltpu.SemaphoreType.DMA((4,)),
            pltpu.SemaphoreType.DMA((7,)),
            pltpu.SemaphoreType.DMA((7,)),
        ],
        compiler_params=pltpu.CompilerParams(
            collective_id=1, has_side_effects=True, vmem_limit_bytes=56 * 1024 * 1024
        ),
        cost_estimate=pl.CostEstimate(
            flops=2 * slots * block * block * pix_local,
            transcendentals=0,
            bytes_accessed=ext_rows * pix_local * 2 + slots * block * block * 4,
        ),
    )(flat, before, local, after, chunk)

MESH = pl.DeviceIdType.MESH


def scatter_kernel(g_ref, e_ref, out_ref, eout_ref, r1, s1, recv_r, recv_l, acc_r, acc_l, tbuf, r3, ebuf, send_sem, recv_sem):
    p = lax.axis_index("pix")
    c = p % 2
    x = (p // 2) % 4
    yl = p // 8
    partner = p + 1 - 2 * c
    right = (yl * 4 + (x + 1) % 4) * 2 + c
    left = (yl * 4 + (x + 3) % 4) * 2 + c
    ypart = ((1 - yl) * 4 + x) * 2 + c

    barrier = pltpu.get_barrier_semaphore()
    for peer in (partner, right, left, ypart):
        pl.semaphore_signal(barrier, 1, device_id={"pix": peer}, device_id_type=MESH)
    pl.semaphore_wait(barrier, 4)

    def remote(src, dst, k, peer):
        return pltpu.make_async_remote_copy(
            src_ref=src, dst_ref=dst, send_sem=send_sem.at[k], recv_sem=recv_sem.at[k],
            device_id={"pix": peer}, device_id_type=MESH,
        )

    c1 = remote(g_ref.at[1 - c], r1, 0, partner)
    c1.start()
    ce1 = remote(e_ref, ebuf.at[0], 1, partner)
    ce1.start()
    c1.wait()
    ce1.wait()
    for j in range(4):
        s1[j] = g_ref[c, j] + r1[j]
    ebuf[1] = e_ref[...] + ebuf[0]

    done = []
    cr = cl = None
    for k in range(3):
        jr = (x + 3 - k) % 4
        jl = (x + k + 1) % 4
        if k == 0:
            src_r, src_l = s1.at[jr, 0], s1.at[jl, 1]
        else:
            cr.wait_recv()
            cl.wait_recv()
            acc_r[k] = s1[jr, 0] + recv_r[k - 1]
            acc_l[k] = s1[jl, 1] + recv_l[k - 1]
            src_r, src_l = acc_r.at[k], acc_l.at[k]
        cr = remote(src_r, recv_r.at[k], 2 + k, right)
        cr.start()
        cl = remote(src_l, recv_l.at[k], 5 + k, left)
        cl.start()
        done += [cr, cl]
        if k == 0:
            er = remote(ebuf.at[1], ebuf.at[2], 8, right)
            er.start()
            el = remote(ebuf.at[1], ebuf.at[3], 9, left)
            el.start()
            done += [er, el]
        if k == 1:
            er.wait_recv()
            ef = remote(ebuf.at[2], ebuf.at[4], 10, right)
            ef.start()
            done.append(ef)
    cr.wait_recv()
    cl.wait_recv()
    tbuf[0] = s1[x, 0] + recv_r[2]
    tbuf[1] = s1[x, 1] + recv_l[2]
    el.wait_recv()
    ef.wait_recv()
    ebuf[5] = ebuf[1] + ebuf[2] + ebuf[3] + ebuf[4]

    c3 = remote(tbuf.at[1 - yl], r3, 11, ypart)
    c3.start()
    ce3 = remote(ebuf.at[5], ebuf.at[6], 12, ypart)
    ce3.start()
    c3.wait()
    ce3.wait()
    out_ref[...] = tbuf[yl] + r3[...]
    eout_ref[...] = ebuf[5] + ebuf[6]
    for d in done:
        d.wait_send()


def scatter_grams(grams, energy_part):
    slots, rows, block = grams.shape[-3:]
    part = (slots, rows, block)
    f32 = jnp.float32
    return pl.pallas_call(
        scatter_kernel,
        out_shape=(
            jax.ShapeDtypeStruct(part, f32),
            jax.ShapeDtypeStruct(energy_part.shape, f32),
        ),
        in_specs=[pl.BlockSpec(memory_space=pltpu.VMEM)] * 2,
        out_specs=(pl.BlockSpec(memory_space=pltpu.VMEM),) * 2,
        scratch_shapes=[
            pltpu.VMEM((4, 2) + part, f32),
            pltpu.VMEM((4, 2) + part, f32),
            pltpu.VMEM((3,) + part, f32),
            pltpu.VMEM((3,) + part, f32),
            pltpu.VMEM((3,) + part, f32),
            pltpu.VMEM((3,) + part, f32),
            pltpu.VMEM((2,) + part, f32),
            pltpu.VMEM(part, f32),
            pltpu.VMEM((7,) + energy_part.shape, f32),
            pltpu.SemaphoreType.DMA((13,)),
            pltpu.SemaphoreType.DMA((13,)),
        ],
        compiler_params=pltpu.CompilerParams(
            collective_id=0, has_side_effects=True, vmem_limit_bytes=48 * 1024 * 1024
        ),
    )(grams, energy_part)


def smooth_rows(padded, stencil):
    pix_local = stencil.shape[1]
    total = jnp.zeros((padded.shape[0], pix_local), jnp.float32)
    for tap in range(5):
        total = total + stencil[tap][None, :] * padded[:, tap : tap + pix_local].astype(jnp.float32)
    return total.astype(jnp.bfloat16)


def row_squares(rows):
    values = rows.astype(jnp.float32)
    return jnp.sum(values * values, axis=1)


def on_device(images, stencil, pairs, live, rule_of_block, adduct):
    local_rows, pix_local = images.shape
    block = adduct.shape[1]
    local_blocks = local_rows // block
    shares = lax.axis_size("pix")
    rows = block // shares
    width = REACH * block
    ions = lax.axis_size("ion")
    up = [(i, i + 1) for i in range(ions - 1)]
    down = [(j, i) for i, j in up]
    raw_before = lax.ppermute(images[local_rows - width :], "ion", up)
    raw_after = lax.ppermute(images[:width], "ion", down)
    me_pix = lax.axis_index("pix")
    offset = me_pix * rows
    me_pix = lax.axis_index("pix")
    me_ion = lax.axis_index("ion")
    per_index = adduct.shape[0]
    turn = [
        (p * ions + j, p * ions + (j - p) % ions)
        for j in range(ions)
        for p in range(1, shares)
    ]
    padded = extended_2(images, (("pix", 1),), 2)
    smoothed = smooth_rows(padded, stencil)
    local_squares = row_squares(smoothed)
    edges = jnp.concatenate([padded[:, :2], padded[:, pix_local + 2 :]], axis=1)
    edges, late_adduct, smoothed, local_squares = lax.optimization_barrier(
        (edges, adduct, smoothed, local_squares)
    )
    fetched = lax.ppermute(late_adduct, ("pix", "ion"), turn)
    own_turn = jnp.where(me_pix == 0, late_adduct, fetched)
    edge_before = lax.ppermute(edges[local_rows - width :], "ion", up)
    edge_after = lax.ppermute(edges[:width], "ion", down)
    before = smooth_rows(
        jnp.concatenate([edge_before[:, :2], raw_before, edge_before[:, 2:]], axis=1), stencil
    )
    after = smooth_rows(
        jnp.concatenate([edge_after[:, :2], raw_after, edge_after[:, 2:]], axis=1), stencil
    )
    squares = jnp.concatenate([row_squares(before), local_squares, row_squares(after)])
    pixel_count = pix_local * shares
    first = lax.axis_index("ion") * local_blocks
    slots = pairs.shape[0]
    relative = pairs - first + REACH

    grams, lookup_tables = pair_grams(relative, before, smoothed, after, own_turn, shares, block)
    lookup_tables = lookup_tables.reshape((-1,) + adduct.shape[1:])
    gram, energy_sum = scatter_grams(grams, squares.reshape(-1, block))
    inverse = 1.0 / jnp.sqrt(energy_sum.reshape(-1) / pixel_count + 1e-06)
    inv_blocks = inverse.reshape(local_blocks + 2 * REACH, block)

    inv_left = lax.dynamic_slice_in_dim(
        jnp.take(inv_blocks, relative[:, 0], axis=0), offset, rows, 1
    )
    inv_right = jnp.take(inv_blocks, relative[:, 1], axis=0)
    rules = jnp.take(rule_of_block, pairs[:, 1], axis=0)
    source = (rules // per_index - me_ion) % ions
    slot = (source % 2) * 8 + ((source // 2) % 4) * 2 + source // 8
    rules = slot * per_index + rules % per_index
    matrices = jnp.take(lookup_tables, rules, axis=0)
    coloc = (gram * inv_left[:, :, None] * inv_right[:, None, :] / pixel_count).astype(jnp.bfloat16)
    scores = jnp.einsum("src,scd->srd", coloc, matrices, preferred_element_type=jnp.float32)
    used = jnp.arange(slots, dtype=jnp.int32) < live[0]
    scores = jnp.where(used[:, None, None], scores, 0.0).astype(jnp.bfloat16)
    return (smoothed, scores)


def solution(mesh):
    return jax.shard_map(
        on_device,
        mesh=mesh,
        in_specs=(
            P("ion", "pix"),
            P(None, "pix"),
            P("ion", None),
            P("ion"),
            P(),
            P("ion", None, None),
        ),
        out_specs=(P("ion", "pix"), P("ion", "pix", None)),
        check_vma=False,
    )
```

```python
import jax
import jax.numpy as jnp
from jax import lax
from jax.experimental import pallas as pl
from jax.experimental.pallas import tpu as pltpu
from jax.sharding import PartitionSpec as P

REACH = 3


def extended_2(array, sides, width):
    for axis, dim in sides:
        size, length = (lax.axis_size(axis), array.shape[dim])
        up = [(i, (i + 1) % size) for i in range(size - 1)]
        down = [(j, i) for i, j in up]
        last = lax.slice_in_dim(array, length - width, length, axis=dim)
        first = lax.slice_in_dim(array, 0, width, axis=dim)
        before = lax.ppermute(last, axis, up)
        after = lax.ppermute(first, axis, down)
        array = jnp.concatenate([before, array, after], axis=dim)
    return array


def gram_kernel(shares, rel_ref, before_ref, local_ref, after_ref, chunk_ref, out_ref, table_out,
                ext_ref, table, sems, send_sems, recv_sems):
    block = out_ref.shape[-1]
    slots = out_ref.shape[-3]
    rows = out_ref.shape[-2]
    width = before_ref.shape[0]
    middle = local_ref.shape[0]
    p = lax.axis_index("pix")
    c = p % 2
    x = (p // 2) % 4
    yl = p // 8
    partner = p + 1 - 2 * c
    right = (yl * 4 + (x + 1) % 4) * 2 + c
    left = (yl * 4 + (x + 3) % 4) * 2 + c
    ypart = ((1 - yl) * 4 + x) * 2 + c
    mine = c * 8 + x * 2 + yl
    theirs = c * 8 + x * 2 + 1 - yl
    pair_at = c * 8 + x * 2
    from_left = c * 8 + ((x + 3) % 4) * 2

    barrier = pltpu.get_barrier_semaphore()
    for peer in (partner, right, left, ypart):
        pl.semaphore_signal(barrier, 1, device_id={"pix": peer}, device_id_type=MESH)
    pl.semaphore_wait(barrier, 4)

    def remote(src, dst, k, peer):
        return pltpu.make_async_remote_copy(
            src_ref=src, dst_ref=dst, send_sem=send_sems.at[k], recv_sem=recv_sems.at[k],
            device_id={"pix": peer}, device_id_type=MESH,
        )

    sent = []
    ca = remote(chunk_ref, table.at[mine], 0, ypart)
    ca.start()
    sent.append(ca)
    own = pltpu.make_async_copy(chunk_ref, table.at[mine], sems.at[3])
    own.start()

    copies = [
        pltpu.make_async_copy(local_ref, ext_ref.at[pl.ds(width, middle)], sems.at[0]),
        pltpu.make_async_copy(before_ref, ext_ref.at[pl.ds(0, width)], sems.at[1]),
        pltpu.make_async_copy(after_ref, ext_ref.at[pl.ds(width + middle, width)], sems.at[2]),
    ]
    for cp in copies:
        cp.start()
    for cp in copies:
        cp.wait()

    def body(s, carry):
        left_rows = ext_ref[rel_ref[2 * s]]
        right_rows = ext_ref[rel_ref[2 * s + 1]]
        g = lax.dot_general(
            left_rows, right_rows, (((1,), (1,)), ((), ())), preferred_element_type=jnp.float32
        )
        for q in range(shares):
            out_ref[q % 2, (q // 2) % 4, q // 8, s] = g[q * rows : (q + 1) * rows, :]
        return carry

    third = slots // 3
    lax.fori_loop(0, third, body, 0)
    ca.wait_recv()
    b1 = [
        remote(chunk_ref, table.at[mine], 1, right),
        remote(table.at[theirs], table.at[theirs], 2, right),
        remote(chunk_ref, table.at[mine], 3, left),
        remote(table.at[theirs], table.at[theirs], 4, left),
    ]
    for cp in b1:
        cp.start()
    sent += b1
    lax.fori_loop(third, 2 * third, body, 0)
    for cp in b1:
        cp.wait_recv()
    b2 = remote(table.at[pl.ds(from_left, 2)], table.at[pl.ds(from_left, 2)], 5, right)
    b2.start()
    sent.append(b2)
    lax.fori_loop(2 * third, slots, body, 0)
    b2.wait_recv()
    own.wait()
    cc = remote(table.at[pl.ds(c * 8, 8)], table.at[pl.ds(c * 8, 8)], 6, partner)
    cc.start()
    sent.append(cc)
    cc.wait_recv()
    for cp in sent:
        cp.wait_send()
    table_out[...] = table[...]


def pair_grams(relative, before, local, after, chunk, shares, block):
    slots = relative.shape[0]
    rows = block // shares
    pix_local = local.shape[1]
    ext_blocks = (before.shape[0] + local.shape[0] + after.shape[0]) // block
    ext_rows = ext_blocks * block
    flat = relative.reshape(-1).astype(jnp.int32)
    table_shape = (shares,) + chunk.shape
    before, local, after = (a.reshape(-1, block, pix_local) for a in (before, local, after))
    return pl.pallas_call(
        lambda *refs: gram_kernel(shares, *refs),
        out_shape=(
            jax.ShapeDtypeStruct((2, 4, 2, slots, rows, block), jnp.float32),
            jax.ShapeDtypeStruct(table_shape, chunk.dtype),
        ),
        in_specs=[pl.BlockSpec(memory_space=pltpu.SMEM)]
        + [pl.BlockSpec(memory_space=pl.ANY)] * 3
        + [pl.BlockSpec(memory_space=pltpu.VMEM)],
        out_specs=(pl.BlockSpec(memory_space=pltpu.VMEM),) * 2,
        scratch_shapes=[
            pltpu.VMEM((ext_blocks, block, pix_local), local.dtype),
            pltpu.VMEM(table_shape, chunk.dtype),
            pltpu.SemaphoreType.DMA((4,)),
            pltpu.SemaphoreType.DMA((7,)),
            pltpu.SemaphoreType.DMA((7,)),
        ],
        compiler_params=pltpu.CompilerParams(
            collective_id=1, has_side_effects=True, vmem_limit_bytes=56 * 1024 * 1024
        ),
        cost_estimate=pl.CostEstimate(
            flops=2 * slots * block * block * pix_local,
            transcendentals=0,
            bytes_accessed=ext_rows * pix_local * 2 + slots * block * block * 4,
        ),
    )(flat, before, local, after, chunk)

MESH = pl.DeviceIdType.MESH


def scatter_kernel(g_ref, e_ref, out_ref, eout_ref, r1, s1, recv_r, recv_l, acc_r, acc_l, tbuf, r3, ebuf, send_sem, recv_sem):
    p = lax.axis_index("pix")
    c = p % 2
    x = (p // 2) % 4
    yl = p // 8
    partner = p + 1 - 2 * c
    right = (yl * 4 + (x + 1) % 4) * 2 + c
    left = (yl * 4 + (x + 3) % 4) * 2 + c
    ypart = ((1 - yl) * 4 + x) * 2 + c

    barrier = pltpu.get_barrier_semaphore()
    for peer in (partner, right, left, ypart):
        pl.semaphore_signal(barrier, 1, device_id={"pix": peer}, device_id_type=MESH)
    pl.semaphore_wait(barrier, 4)

    def remote(src, dst, k, peer):
        return pltpu.make_async_remote_copy(
            src_ref=src, dst_ref=dst, send_sem=send_sem.at[k], recv_sem=recv_sem.at[k],
            device_id={"pix": peer}, device_id_type=MESH,
        )

    c1 = remote(g_ref.at[1 - c], r1, 0, partner)
    c1.start()
    ce1 = remote(e_ref, ebuf.at[0], 1, partner)
    ce1.start()
    c1.wait()
    ce1.wait()
    for j in range(4):
        s1[j] = g_ref[c, j] + r1[j]
    ebuf[1] = e_ref[...] + ebuf[0]

    done = []
    cr = cl = None
    for k in range(3):
        jr = (x + 3 - k) % 4
        jl = (x + k + 1) % 4
        if k == 0:
            src_r, src_l = s1.at[jr, 0], s1.at[jl, 1]
        else:
            cr.wait_recv()
            cl.wait_recv()
            acc_r[k] = s1[jr, 0] + recv_r[k - 1]
            acc_l[k] = s1[jl, 1] + recv_l[k - 1]
            src_r, src_l = acc_r.at[k], acc_l.at[k]
        cr = remote(src_r, recv_r.at[k], 2 + k, right)
        cr.start()
        cl = remote(src_l, recv_l.at[k], 5 + k, left)
        cl.start()
        done += [cr, cl]
        if k == 0:
            er = remote(ebuf.at[1], ebuf.at[2], 8, right)
            er.start()
            el = remote(ebuf.at[1], ebuf.at[3], 9, left)
            el.start()
            done += [er, el]
        if k == 1:
            er.wait_recv()
            ef = remote(ebuf.at[2], ebuf.at[4], 10, right)
            ef.start()
            done.append(ef)
    cr.wait_recv()
    cl.wait_recv()
    tbuf[0] = s1[x, 0] + recv_r[2]
    tbuf[1] = s1[x, 1] + recv_l[2]
    el.wait_recv()
    ef.wait_recv()
    ebuf[5] = ebuf[1] + ebuf[2] + ebuf[3] + ebuf[4]

    c3 = remote(tbuf.at[1 - yl], r3, 11, ypart)
    c3.start()
    ce3 = remote(ebuf.at[5], ebuf.at[6], 12, ypart)
    ce3.start()
    c3.wait()
    ce3.wait()
    out_ref[...] = tbuf[yl] + r3[...]
    eout_ref[...] = ebuf[5] + ebuf[6]
    for d in done:
        d.wait_send()


def scatter_grams(grams, energy_part):
    slots, rows, block = grams.shape[-3:]
    part = (slots, rows, block)
    f32 = jnp.float32
    return pl.pallas_call(
        scatter_kernel,
        out_shape=(
            jax.ShapeDtypeStruct(part, f32),
            jax.ShapeDtypeStruct(energy_part.shape, f32),
        ),
        in_specs=[pl.BlockSpec(memory_space=pltpu.VMEM)] * 2,
        out_specs=(pl.BlockSpec(memory_space=pltpu.VMEM),) * 2,
        scratch_shapes=[
            pltpu.VMEM((4, 2) + part, f32),
            pltpu.VMEM((4, 2) + part, f32),
            pltpu.VMEM((3,) + part, f32),
            pltpu.VMEM((3,) + part, f32),
            pltpu.VMEM((3,) + part, f32),
            pltpu.VMEM((3,) + part, f32),
            pltpu.VMEM((2,) + part, f32),
            pltpu.VMEM(part, f32),
            pltpu.VMEM((7,) + energy_part.shape, f32),
            pltpu.SemaphoreType.DMA((13,)),
            pltpu.SemaphoreType.DMA((13,)),
        ],
        compiler_params=pltpu.CompilerParams(
            collective_id=0, has_side_effects=True, vmem_limit_bytes=48 * 1024 * 1024
        ),
    )(grams, energy_part)


def smooth_rows(padded, stencil):
    pix_local = stencil.shape[1]
    total = jnp.zeros((padded.shape[0], pix_local), jnp.float32)
    for tap in range(5):
        total = total + stencil[tap][None, :] * padded[:, tap : tap + pix_local].astype(jnp.float32)
    return total.astype(jnp.bfloat16)


def row_squares(rows):
    values = rows.astype(jnp.float32)
    return jnp.sum(values * values, axis=1)


def on_device(images, stencil, pairs, live, rule_of_block, adduct):
    local_rows, pix_local = images.shape
    block = adduct.shape[1]
    local_blocks = local_rows // block
    shares = lax.axis_size("pix")
    rows = block // shares
    width = REACH * block
    ions = lax.axis_size("ion")
    up = [(i, i + 1) for i in range(ions - 1)]
    down = [(j, i) for i, j in up]
    raw_before = lax.ppermute(images[local_rows - width :], "ion", up)
    raw_after = lax.ppermute(images[:width], "ion", down)
    me_pix = lax.axis_index("pix")
    offset = me_pix * rows
    me_pix = lax.axis_index("pix")
    me_ion = lax.axis_index("ion")
    per_index = adduct.shape[0]
    turn = [
        (p * ions + j, p * ions + (j - p) % ions)
        for j in range(ions)
        for p in range(1, shares)
    ]
    fetched = lax.ppermute(adduct, ("pix", "ion"), turn)
    own_turn = jnp.where(me_pix == 0, adduct, fetched)
    padded = extended_2(images, (("pix", 1),), 2)
    smoothed = smooth_rows(padded, stencil)
    local_squares = row_squares(smoothed)
    edges = jnp.concatenate([padded[:, :2], padded[:, pix_local + 2 :]], axis=1)
    edges, smoothed, local_squares = lax.optimization_barrier((edges, smoothed, local_squares))
    edge_before = lax.ppermute(edges[local_rows - width :], "ion", up)
    edge_after = lax.ppermute(edges[:width], "ion", down)
    before = smooth_rows(
        jnp.concatenate([edge_before[:, :2], raw_before, edge_before[:, 2:]], axis=1), stencil
    )
    after = smooth_rows(
        jnp.concatenate([edge_after[:, :2], raw_after, edge_after[:, 2:]], axis=1), stencil
    )
    squares = jnp.concatenate([row_squares(before), local_squares, row_squares(after)])
    pixel_count = pix_local * shares
    first = lax.axis_index("ion") * local_blocks
    slots = pairs.shape[0]
    relative = pairs - first + REACH

    grams, lookup_tables = pair_grams(relative, before, smoothed, after, own_turn, shares, block)
    lookup_tables = lookup_tables.reshape((-1,) + adduct.shape[1:])
    gram, energy_sum = scatter_grams(grams, squares.reshape(-1, block))
    inverse = 1.0 / jnp.sqrt(energy_sum.reshape(-1) / pixel_count + 1e-06)
    inv_blocks = inverse.reshape(local_blocks + 2 * REACH, block)

    inv_left = lax.dynamic_slice_in_dim(
        jnp.take(inv_blocks, relative[:, 0], axis=0), offset, rows, 1
    )
    inv_right = jnp.take(inv_blocks, relative[:, 1], axis=0)
    rules = jnp.take(rule_of_block, pairs[:, 1], axis=0)
    source = (rules // per_index - me_ion) % ions
    slot = (source % 2) * 8 + ((source // 2) % 4) * 2 + source // 8
    rules = slot * per_index + rules % per_index
    matrices = jnp.take(lookup_tables, rules, axis=0)
    coloc = (gram * inv_left[:, :, None] * inv_right[:, None, :] / pixel_count).astype(jnp.bfloat16)
    scores = jnp.einsum("src,scd->srd", coloc, matrices, preferred_element_type=jnp.float32)
    used = jnp.arange(slots, dtype=jnp.int32) < live[0]
    scores = jnp.where(used[:, None, None], scores, 0.0).astype(jnp.bfloat16)
    return (smoothed, scores)


def solution(mesh):
    return jax.shard_map(
        on_device,
        mesh=mesh,
        in_specs=(
            P("ion", "pix"),
            P(None, "pix"),
            P("ion", None),
            P("ion"),
            P(),
            P("ion", None, None),
        ),
        out_specs=(P("ion", "pix"), P("ion", "pix", None)),
        check_vma=False,
    )
```

```python
import jax
import jax.numpy as jnp
from jax import lax
from jax.experimental import pallas as pl
from jax.experimental.pallas import tpu as pltpu
from jax.sharding import PartitionSpec as P

REACH = 3


def extended_2(array, sides, width):
    for axis, dim in sides:
        size, length = (lax.axis_size(axis), array.shape[dim])
        up = [(i, (i + 1) % size) for i in range(size - 1)]
        down = [(j, i) for i, j in up]
        last = lax.slice_in_dim(array, length - width, length, axis=dim)
        first = lax.slice_in_dim(array, 0, width, axis=dim)
        before = lax.ppermute(last, axis, up)
        after = lax.ppermute(first, axis, down)
        array = jnp.concatenate([before, array, after], axis=dim)
    return array


def gram_kernel(shares, rel_ref, before_ref, local_ref, after_ref, chunk_ref, out_ref, table_out,
                ext_ref, table, sems, send_sems, recv_sems):
    block = out_ref.shape[-1]
    slots = out_ref.shape[-3]
    rows = out_ref.shape[-2]
    width = before_ref.shape[0]
    middle = local_ref.shape[0]
    p = lax.axis_index("pix")
    c = p % 2
    x = (p // 2) % 4
    yl = p // 8
    partner = p + 1 - 2 * c
    right = (yl * 4 + (x + 1) % 4) * 2 + c
    left = (yl * 4 + (x + 3) % 4) * 2 + c
    ypart = ((1 - yl) * 4 + x) * 2 + c
    mine = c * 8 + x * 2 + yl
    theirs = c * 8 + x * 2 + 1 - yl
    pair_at = c * 8 + x * 2
    from_left = c * 8 + ((x + 3) % 4) * 2

    barrier = pltpu.get_barrier_semaphore()
    for peer in (partner, right, left, ypart):
        pl.semaphore_signal(barrier, 1, device_id={"pix": peer}, device_id_type=MESH)
    pl.semaphore_wait(barrier, 4)

    def remote(src, dst, k, peer):
        return pltpu.make_async_remote_copy(
            src_ref=src, dst_ref=dst, send_sem=send_sems.at[k], recv_sem=recv_sems.at[k],
            device_id={"pix": peer}, device_id_type=MESH,
        )

    sent = []
    ca = remote(chunk_ref, table.at[mine], 0, ypart)
    ca.start()
    sent.append(ca)
    own = pltpu.make_async_copy(chunk_ref, table.at[mine], sems.at[3])
    own.start()

    copies = [
        pltpu.make_async_copy(local_ref, ext_ref.at[pl.ds(width, middle)], sems.at[0]),
        pltpu.make_async_copy(before_ref, ext_ref.at[pl.ds(0, width)], sems.at[1]),
        pltpu.make_async_copy(after_ref, ext_ref.at[pl.ds(width + middle, width)], sems.at[2]),
    ]
    for cp in copies:
        cp.start()
    for cp in copies:
        cp.wait()

    def body(s, carry):
        left_rows = ext_ref[rel_ref[2 * s]]
        right_rows = ext_ref[rel_ref[2 * s + 1]]
        g = lax.dot_general(
            left_rows, right_rows, (((1,), (1,)), ((), ())), preferred_element_type=jnp.float32
        )
        for q in range(shares):
            out_ref[q % 2, (q // 2) % 4, q // 8, s] = g[q * rows : (q + 1) * rows, :]
        return carry

    third = slots // 4
    lax.fori_loop(0, third, body, 0)
    ca.wait_recv()
    b1 = [
        remote(chunk_ref, table.at[mine], 1, right),
        remote(table.at[theirs], table.at[theirs], 2, right),
        remote(chunk_ref, table.at[mine], 3, left),
        remote(table.at[theirs], table.at[theirs], 4, left),
    ]
    for cp in b1:
        cp.start()
    sent += b1
    lax.fori_loop(third, 2 * third, body, 0)
    for cp in b1:
        cp.wait_recv()
    b2 = remote(table.at[pl.ds(from_left, 2)], table.at[pl.ds(from_left, 2)], 5, right)
    b2.start()
    sent.append(b2)
    lax.fori_loop(2 * third, 3 * third, body, 0)
    b2.wait_recv()
    own.wait()
    cc = remote(table.at[pl.ds(c * 8, 8)], table.at[pl.ds(c * 8, 8)], 6, partner)
    cc.start()
    sent.append(cc)
    lax.fori_loop(3 * third, slots, body, 0)
    cc.wait_recv()
    for cp in sent:
        cp.wait_send()
    table_out[...] = table[...]


def pair_grams(relative, before, local, after, chunk, shares, block):
    slots = relative.shape[0]
    rows = block // shares
    pix_local = local.shape[1]
    ext_blocks = (before.shape[0] + local.shape[0] + after.shape[0]) // block
    ext_rows = ext_blocks * block
    flat = relative.reshape(-1).astype(jnp.int32)
    table_shape = (shares,) + chunk.shape
    before, local, after = (a.reshape(-1, block, pix_local) for a in (before, local, after))
    return pl.pallas_call(
        lambda *refs: gram_kernel(shares, *refs),
        out_shape=(
            jax.ShapeDtypeStruct((2, 4, 2, slots, rows, block), jnp.float32),
            jax.ShapeDtypeStruct(table_shape, chunk.dtype),
        ),
        in_specs=[pl.BlockSpec(memory_space=pltpu.SMEM)]
        + [pl.BlockSpec(memory_space=pl.ANY)] * 3
        + [pl.BlockSpec(memory_space=pltpu.VMEM)],
        out_specs=(pl.BlockSpec(memory_space=pltpu.VMEM),) * 2,
        scratch_shapes=[
            pltpu.VMEM((ext_blocks, block, pix_local), local.dtype),
            pltpu.VMEM(table_shape, chunk.dtype),
            pltpu.SemaphoreType.DMA((4,)),
            pltpu.SemaphoreType.DMA((7,)),
            pltpu.SemaphoreType.DMA((7,)),
        ],
        compiler_params=pltpu.CompilerParams(
            collective_id=1, has_side_effects=True, vmem_limit_bytes=56 * 1024 * 1024
        ),
        cost_estimate=pl.CostEstimate(
            flops=2 * slots * block * block * pix_local,
            transcendentals=0,
            bytes_accessed=ext_rows * pix_local * 2 + slots * block * block * 4,
        ),
    )(flat, before, local, after, chunk)

MESH = pl.DeviceIdType.MESH


def scatter_kernel(g_ref, e_ref, out_ref, eout_ref, r1, s1, recv_r, recv_l, acc_r, acc_l, tbuf, r3, ebuf, send_sem, recv_sem):
    p = lax.axis_index("pix")
    c = p % 2
    x = (p // 2) % 4
    yl = p // 8
    partner = p + 1 - 2 * c
    right = (yl * 4 + (x + 1) % 4) * 2 + c
    left = (yl * 4 + (x + 3) % 4) * 2 + c
    ypart = ((1 - yl) * 4 + x) * 2 + c

    barrier = pltpu.get_barrier_semaphore()
    for peer in (partner, right, left, ypart):
        pl.semaphore_signal(barrier, 1, device_id={"pix": peer}, device_id_type=MESH)
    pl.semaphore_wait(barrier, 4)

    def remote(src, dst, k, peer):
        return pltpu.make_async_remote_copy(
            src_ref=src, dst_ref=dst, send_sem=send_sem.at[k], recv_sem=recv_sem.at[k],
            device_id={"pix": peer}, device_id_type=MESH,
        )

    c1 = remote(g_ref.at[1 - c], r1, 0, partner)
    c1.start()
    ce1 = remote(e_ref, ebuf.at[0], 1, partner)
    ce1.start()
    c1.wait()
    ce1.wait()
    for j in range(4):
        s1[j] = g_ref[c, j] + r1[j]
    ebuf[1] = e_ref[...] + ebuf[0]

    done = []
    cr = cl = None
    for k in range(3):
        jr = (x + 3 - k) % 4
        jl = (x + k + 1) % 4
        if k == 0:
            src_r, src_l = s1.at[jr, 0], s1.at[jl, 1]
        else:
            cr.wait_recv()
            cl.wait_recv()
            acc_r[k] = s1[jr, 0] + recv_r[k - 1]
            acc_l[k] = s1[jl, 1] + recv_l[k - 1]
            src_r, src_l = acc_r.at[k], acc_l.at[k]
        cr = remote(src_r, recv_r.at[k], 2 + k, right)
        cr.start()
        cl = remote(src_l, recv_l.at[k], 5 + k, left)
        cl.start()
        done += [cr, cl]
        if k == 0:
            er = remote(ebuf.at[1], ebuf.at[2], 8, right)
            er.start()
            el = remote(ebuf.at[1], ebuf.at[3], 9, left)
            el.start()
            done += [er, el]
        if k == 1:
            er.wait_recv()
            ef = remote(ebuf.at[2], ebuf.at[4], 10, right)
            ef.start()
            done.append(ef)
    cr.wait_recv()
    cl.wait_recv()
    tbuf[0] = s1[x, 0] + recv_r[2]
    tbuf[1] = s1[x, 1] + recv_l[2]
    el.wait_recv()
    ef.wait_recv()
    ebuf[5] = ebuf[1] + ebuf[2] + ebuf[3] + ebuf[4]

    c3 = remote(tbuf.at[1 - yl], r3, 11, ypart)
    c3.start()
    ce3 = remote(ebuf.at[5], ebuf.at[6], 12, ypart)
    ce3.start()
    c3.wait()
    ce3.wait()
    out_ref[...] = tbuf[yl] + r3[...]
    eout_ref[...] = ebuf[5] + ebuf[6]
    for d in done:
        d.wait_send()


def scatter_grams(grams, energy_part):
    slots, rows, block = grams.shape[-3:]
    part = (slots, rows, block)
    f32 = jnp.float32
    return pl.pallas_call(
        scatter_kernel,
        out_shape=(
            jax.ShapeDtypeStruct(part, f32),
            jax.ShapeDtypeStruct(energy_part.shape, f32),
        ),
        in_specs=[pl.BlockSpec(memory_space=pltpu.VMEM)] * 2,
        out_specs=(pl.BlockSpec(memory_space=pltpu.VMEM),) * 2,
        scratch_shapes=[
            pltpu.VMEM((4, 2) + part, f32),
            pltpu.VMEM((4, 2) + part, f32),
            pltpu.VMEM((3,) + part, f32),
            pltpu.VMEM((3,) + part, f32),
            pltpu.VMEM((3,) + part, f32),
            pltpu.VMEM((3,) + part, f32),
            pltpu.VMEM((2,) + part, f32),
            pltpu.VMEM(part, f32),
            pltpu.VMEM((7,) + energy_part.shape, f32),
            pltpu.SemaphoreType.DMA((13,)),
            pltpu.SemaphoreType.DMA((13,)),
        ],
        compiler_params=pltpu.CompilerParams(
            collective_id=0, has_side_effects=True, vmem_limit_bytes=48 * 1024 * 1024
        ),
    )(grams, energy_part)


def smooth_rows(padded, stencil):
    pix_local = stencil.shape[1]
    total = jnp.zeros((padded.shape[0], pix_local), jnp.float32)
    for tap in range(5):
        total = total + stencil[tap][None, :] * padded[:, tap : tap + pix_local].astype(jnp.float32)
    return total.astype(jnp.bfloat16)


def row_squares(rows):
    values = rows.astype(jnp.float32)
    return jnp.sum(values * values, axis=1)


def on_device(images, stencil, pairs, live, rule_of_block, adduct):
    local_rows, pix_local = images.shape
    block = adduct.shape[1]
    local_blocks = local_rows // block
    shares = lax.axis_size("pix")
    rows = block // shares
    width = REACH * block
    ions = lax.axis_size("ion")
    up = [(i, i + 1) for i in range(ions - 1)]
    down = [(j, i) for i, j in up]
    raw_before = lax.ppermute(images[local_rows - width :], "ion", up)
    raw_after = lax.ppermute(images[:width], "ion", down)
    me_pix = lax.axis_index("pix")
    offset = me_pix * rows
    me_pix = lax.axis_index("pix")
    me_ion = lax.axis_index("ion")
    per_index = adduct.shape[0]
    turn = [
        (p * ions + j, p * ions + (j - p) % ions)
        for j in range(ions)
        for p in range(1, shares)
    ]
    fetched = lax.ppermute(adduct, ("pix", "ion"), turn)
    own_turn = jnp.where(me_pix == 0, adduct, fetched)
    padded = extended_2(images, (("pix", 1),), 2)
    smoothed = smooth_rows(padded, stencil)
    local_squares = row_squares(smoothed)
    edges = jnp.concatenate([padded[:, :2], padded[:, pix_local + 2 :]], axis=1)
    edge_before = lax.ppermute(edges[local_rows - width :], "ion", up)
    edge_after = lax.ppermute(edges[:width], "ion", down)
    before = smooth_rows(
        jnp.concatenate([edge_before[:, :2], raw_before, edge_before[:, 2:]], axis=1), stencil
    )
    after = smooth_rows(
        jnp.concatenate([edge_after[:, :2], raw_after, edge_after[:, 2:]], axis=1), stencil
    )
    squares = jnp.concatenate([row_squares(before), local_squares, row_squares(after)])
    pixel_count = pix_local * shares
    first = lax.axis_index("ion") * local_blocks
    slots = pairs.shape[0]
    relative = pairs - first + REACH

    grams, lookup_tables = pair_grams(relative, before, smoothed, after, own_turn, shares, block)
    lookup_tables = lookup_tables.reshape((-1,) + adduct.shape[1:])
    gram, energy_sum = scatter_grams(grams, squares.reshape(-1, block))
    inverse = 1.0 / jnp.sqrt(energy_sum.reshape(-1) / pixel_count + 1e-06)
    inv_blocks = inverse.reshape(local_blocks + 2 * REACH, block)

    inv_left = lax.dynamic_slice_in_dim(
        jnp.take(inv_blocks, relative[:, 0], axis=0), offset, rows, 1
    )
    inv_right = jnp.take(inv_blocks, relative[:, 1], axis=0)
    rules = jnp.take(rule_of_block, pairs[:, 1], axis=0)
    source = (rules // per_index - me_ion) % ions
    slot = (source % 2) * 8 + ((source // 2) % 4) * 2 + source // 8
    rules = slot * per_index + rules % per_index
    matrices = jnp.take(lookup_tables, rules, axis=0)
    coloc = (gram * inv_left[:, :, None] * inv_right[:, None, :] / pixel_count).astype(jnp.bfloat16)
    scores = jnp.einsum("src,scd->srd", coloc, matrices, preferred_element_type=jnp.float32)
    used = jnp.arange(slots, dtype=jnp.int32) < live[0]
    scores = jnp.where(used[:, None, None], scores, 0.0).astype(jnp.bfloat16)
    return (smoothed, scores)


def solution(mesh):
    return jax.shard_map(
        on_device,
        mesh=mesh,
        in_specs=(
            P("ion", "pix"),
            P(None, "pix"),
            P("ion", None),
            P("ion"),
            P(),
            P("ion", None, None),
        ),
        out_specs=(P("ion", "pix"), P("ion", "pix", None)),
        check_vma=False,
    )
```

```python
import jax
import jax.numpy as jnp
from jax import lax
from jax.experimental import pallas as pl
from jax.experimental.pallas import tpu as pltpu
from jax.sharding import PartitionSpec as P

REACH = 3


def extended_2(array, sides, width):
    for axis, dim in sides:
        size, length = (lax.axis_size(axis), array.shape[dim])
        up = [(i, (i + 1) % size) for i in range(size - 1)]
        down = [(j, i) for i, j in up]
        last = lax.slice_in_dim(array, length - width, length, axis=dim)
        first = lax.slice_in_dim(array, 0, width, axis=dim)
        before = lax.ppermute(last, axis, up)
        after = lax.ppermute(first, axis, down)
        array = jnp.concatenate([before, array, after], axis=dim)
    return array


def gram_kernel(shares, rel_ref, before_ref, local_ref, after_ref, chunk_ref, out_ref, table_out,
                ext_ref, table, sems, send_sems, recv_sems):
    block = out_ref.shape[-1]
    slots = out_ref.shape[-3]
    rows = out_ref.shape[-2]
    width = before_ref.shape[0]
    middle = local_ref.shape[0]
    p = lax.axis_index("pix")
    c = p % 2
    x = (p // 2) % 4
    yl = p // 8
    partner = p + 1 - 2 * c
    right = (yl * 4 + (x + 1) % 4) * 2 + c
    left = (yl * 4 + (x + 3) % 4) * 2 + c
    ypart = ((1 - yl) * 4 + x) * 2 + c
    mine = c * 8 + x * 2 + yl
    theirs = c * 8 + x * 2 + 1 - yl
    pair_at = c * 8 + x * 2
    from_left = c * 8 + ((x + 3) % 4) * 2

    barrier = pltpu.get_barrier_semaphore()
    for peer in (partner, right, left, ypart):
        pl.semaphore_signal(barrier, 1, device_id={"pix": peer}, device_id_type=MESH)
    pl.semaphore_wait(barrier, 4)

    def remote(src, dst, k, peer):
        return pltpu.make_async_remote_copy(
            src_ref=src, dst_ref=dst, send_sem=send_sems.at[k], recv_sem=recv_sems.at[k],
            device_id={"pix": peer}, device_id_type=MESH,
        )

    sent = []
    ca = remote(chunk_ref, table.at[mine], 0, ypart)
    ca.start()
    sent.append(ca)
    own = pltpu.make_async_copy(chunk_ref, table.at[mine], sems.at[3])
    own.start()

    copies = [
        pltpu.make_async_copy(local_ref, ext_ref.at[pl.ds(width, middle)], sems.at[0]),
        pltpu.make_async_copy(before_ref, ext_ref.at[pl.ds(0, width)], sems.at[1]),
        pltpu.make_async_copy(after_ref, ext_ref.at[pl.ds(width + middle, width)], sems.at[2]),
    ]
    for cp in copies:
        cp.start()
    for cp in copies:
        cp.wait()

    def body(t, carry):
        left_rows = jnp.concatenate([ext_ref[rel_ref[4 * t]], ext_ref[rel_ref[4 * t + 2]]], axis=0)
        right_rows = jnp.concatenate([ext_ref[rel_ref[4 * t + 1]], ext_ref[rel_ref[4 * t + 3]]], axis=0)
        g = lax.dot_general(
            left_rows, right_rows, (((1,), (1,)), ((), ())), preferred_element_type=jnp.float32
        )
        for half in range(2):
            part = g[half * block : (half + 1) * block, half * block : (half + 1) * block]
            for q in range(shares):
                out_ref[q % 2, (q // 2) % 4, q // 8, 2 * t + half] = part[q * rows : (q + 1) * rows, :]
        return carry

    third = slots // 8
    lax.fori_loop(0, third, body, 0)
    ca.wait_recv()
    b1 = [
        remote(chunk_ref, table.at[mine], 1, right),
        remote(table.at[theirs], table.at[theirs], 2, right),
        remote(chunk_ref, table.at[mine], 3, left),
        remote(table.at[theirs], table.at[theirs], 4, left),
    ]
    for cp in b1:
        cp.start()
    sent += b1
    lax.fori_loop(third, 2 * third, body, 0)
    for cp in b1:
        cp.wait_recv()
    b2 = remote(table.at[pl.ds(from_left, 2)], table.at[pl.ds(from_left, 2)], 5, right)
    b2.start()
    sent.append(b2)
    lax.fori_loop(2 * third, 3 * third, body, 0)
    b2.wait_recv()
    own.wait()
    cc = remote(table.at[pl.ds(c * 8, 8)], table.at[pl.ds(c * 8, 8)], 6, partner)
    cc.start()
    sent.append(cc)
    lax.fori_loop(3 * third, slots // 2, body, 0)
    cc.wait_recv()
    for cp in sent:
        cp.wait_send()
    table_out[...] = table[...]


def pair_grams(relative, before, local, after, chunk, shares, block):
    slots = relative.shape[0]
    rows = block // shares
    pix_local = local.shape[1]
    ext_blocks = (before.shape[0] + local.shape[0] + after.shape[0]) // block
    ext_rows = ext_blocks * block
    flat = relative.reshape(-1).astype(jnp.int32)
    table_shape = (shares,) + chunk.shape
    before, local, after = (a.reshape(-1, block, pix_local) for a in (before, local, after))
    return pl.pallas_call(
        lambda *refs: gram_kernel(shares, *refs),
        out_shape=(
            jax.ShapeDtypeStruct((2, 4, 2, slots, rows, block), jnp.float32),
            jax.ShapeDtypeStruct(table_shape, chunk.dtype),
        ),
        in_specs=[pl.BlockSpec(memory_space=pltpu.SMEM)]
        + [pl.BlockSpec(memory_space=pl.ANY)] * 3
        + [pl.BlockSpec(memory_space=pltpu.VMEM)],
        out_specs=(pl.BlockSpec(memory_space=pltpu.VMEM),) * 2,
        scratch_shapes=[
            pltpu.VMEM((ext_blocks, block, pix_local), local.dtype),
            pltpu.VMEM(table_shape, chunk.dtype),
            pltpu.SemaphoreType.DMA((4,)),
            pltpu.SemaphoreType.DMA((7,)),
            pltpu.SemaphoreType.DMA((7,)),
        ],
        compiler_params=pltpu.CompilerParams(
            collective_id=1, has_side_effects=True, vmem_limit_bytes=56 * 1024 * 1024
        ),
        cost_estimate=pl.CostEstimate(
            flops=2 * slots * block * block * pix_local,
            transcendentals=0,
            bytes_accessed=ext_rows * pix_local * 2 + slots * block * block * 4,
        ),
    )(flat, before, local, after, chunk)

MESH = pl.DeviceIdType.MESH


def scatter_kernel(g_ref, e_ref, out_ref, eout_ref, r1, s1, recv_r, recv_l, acc_r, acc_l, tbuf, r3, ebuf, send_sem, recv_sem):
    p = lax.axis_index("pix")
    c = p % 2
    x = (p // 2) % 4
    yl = p // 8
    partner = p + 1 - 2 * c
    right = (yl * 4 + (x + 1) % 4) * 2 + c
    left = (yl * 4 + (x + 3) % 4) * 2 + c
    ypart = ((1 - yl) * 4 + x) * 2 + c

    barrier = pltpu.get_barrier_semaphore()
    for peer in (partner, right, left, ypart):
        pl.semaphore_signal(barrier, 1, device_id={"pix": peer}, device_id_type=MESH)
    pl.semaphore_wait(barrier, 4)

    def remote(src, dst, k, peer):
        return pltpu.make_async_remote_copy(
            src_ref=src, dst_ref=dst, send_sem=send_sem.at[k], recv_sem=recv_sem.at[k],
            device_id={"pix": peer}, device_id_type=MESH,
        )

    c1 = remote(g_ref.at[1 - c], r1, 0, partner)
    c1.start()
    ce1 = remote(e_ref, ebuf.at[0], 1, partner)
    ce1.start()
    c1.wait()
    ce1.wait()
    for j in range(4):
        s1[j] = g_ref[c, j] + r1[j]
    ebuf[1] = e_ref[...] + ebuf[0]

    done = []
    cr = cl = None
    for k in range(3):
        jr = (x + 3 - k) % 4
        jl = (x + k + 1) % 4
        if k == 0:
            src_r, src_l = s1.at[jr, 0], s1.at[jl, 1]
        else:
            cr.wait_recv()
            cl.wait_recv()
            acc_r[k] = s1[jr, 0] + recv_r[k - 1]
            acc_l[k] = s1[jl, 1] + recv_l[k - 1]
            src_r, src_l = acc_r.at[k], acc_l.at[k]
        cr = remote(src_r, recv_r.at[k], 2 + k, right)
        cr.start()
        cl = remote(src_l, recv_l.at[k], 5 + k, left)
        cl.start()
        done += [cr, cl]
        if k == 0:
            er = remote(ebuf.at[1], ebuf.at[2], 8, right)
            er.start()
            el = remote(ebuf.at[1], ebuf.at[3], 9, left)
            el.start()
            done += [er, el]
        if k == 1:
            er.wait_recv()
            ef = remote(ebuf.at[2], ebuf.at[4], 10, right)
            ef.start()
            done.append(ef)
    cr.wait_recv()
    cl.wait_recv()
    tbuf[0] = s1[x, 0] + recv_r[2]
    tbuf[1] = s1[x, 1] + recv_l[2]
    el.wait_recv()
    ef.wait_recv()
    ebuf[5] = ebuf[1] + ebuf[2] + ebuf[3] + ebuf[4]

    c3 = remote(tbuf.at[1 - yl], r3, 11, ypart)
    c3.start()
    ce3 = remote(ebuf.at[5], ebuf.at[6], 12, ypart)
    ce3.start()
    c3.wait()
    ce3.wait()
    out_ref[...] = tbuf[yl] + r3[...]
    eout_ref[...] = ebuf[5] + ebuf[6]
    for d in done:
        d.wait_send()


def scatter_grams(grams, energy_part):
    slots, rows, block = grams.shape[-3:]
    part = (slots, rows, block)
    f32 = jnp.float32
    return pl.pallas_call(
        scatter_kernel,
        out_shape=(
            jax.ShapeDtypeStruct(part, f32),
            jax.ShapeDtypeStruct(energy_part.shape, f32),
        ),
        in_specs=[pl.BlockSpec(memory_space=pltpu.VMEM)] * 2,
        out_specs=(pl.BlockSpec(memory_space=pltpu.VMEM),) * 2,
        scratch_shapes=[
            pltpu.VMEM((4, 2) + part, f32),
            pltpu.VMEM((4, 2) + part, f32),
            pltpu.VMEM((3,) + part, f32),
            pltpu.VMEM((3,) + part, f32),
            pltpu.VMEM((3,) + part, f32),
            pltpu.VMEM((3,) + part, f32),
            pltpu.VMEM((2,) + part, f32),
            pltpu.VMEM(part, f32),
            pltpu.VMEM((7,) + energy_part.shape, f32),
            pltpu.SemaphoreType.DMA((13,)),
            pltpu.SemaphoreType.DMA((13,)),
        ],
        compiler_params=pltpu.CompilerParams(
            collective_id=0, has_side_effects=True, vmem_limit_bytes=48 * 1024 * 1024
        ),
    )(grams, energy_part)


def smooth_rows(padded, stencil):
    pix_local = stencil.shape[1]
    total = jnp.zeros((padded.shape[0], pix_local), jnp.float32)
    for tap in range(5):
        total = total + stencil[tap][None, :] * padded[:, tap : tap + pix_local].astype(jnp.float32)
    return total.astype(jnp.bfloat16)


def row_squares(rows):
    values = rows.astype(jnp.float32)
    return jnp.sum(values * values, axis=1)


def on_device(images, stencil, pairs, live, rule_of_block, adduct):
    local_rows, pix_local = images.shape
    block = adduct.shape[1]
    local_blocks = local_rows // block
    shares = lax.axis_size("pix")
    rows = block // shares
    width = REACH * block
    ions = lax.axis_size("ion")
    up = [(i, i + 1) for i in range(ions - 1)]
    down = [(j, i) for i, j in up]
    raw_before = lax.ppermute(images[local_rows - width :], "ion", up)
    raw_after = lax.ppermute(images[:width], "ion", down)
    me_pix = lax.axis_index("pix")
    offset = me_pix * rows
    me_pix = lax.axis_index("pix")
    me_ion = lax.axis_index("ion")
    per_index = adduct.shape[0]
    turn = [
        (p * ions + j, p * ions + (j - p) % ions)
        for j in range(ions)
        for p in range(1, shares)
    ]
    fetched = lax.ppermute(adduct, ("pix", "ion"), turn)
    own_turn = jnp.where(me_pix == 0, adduct, fetched)
    padded = extended_2(images, (("pix", 1),), 2)
    smoothed = smooth_rows(padded, stencil)
    local_squares = row_squares(smoothed)
    edges = jnp.concatenate([padded[:, :2], padded[:, pix_local + 2 :]], axis=1)
    edge_before = lax.ppermute(edges[local_rows - width :], "ion", up)
    edge_after = lax.ppermute(edges[:width], "ion", down)
    before = smooth_rows(
        jnp.concatenate([edge_before[:, :2], raw_before, edge_before[:, 2:]], axis=1), stencil
    )
    after = smooth_rows(
        jnp.concatenate([edge_after[:, :2], raw_after, edge_after[:, 2:]], axis=1), stencil
    )
    squares = jnp.concatenate([row_squares(before), local_squares, row_squares(after)])
    pixel_count = pix_local * shares
    first = lax.axis_index("ion") * local_blocks
    slots = pairs.shape[0]
    relative = pairs - first + REACH

    grams, lookup_tables = pair_grams(relative, before, smoothed, after, own_turn, shares, block)
    lookup_tables = lookup_tables.reshape((-1,) + adduct.shape[1:])
    gram, energy_sum = scatter_grams(grams, squares.reshape(-1, block))
    inverse = 1.0 / jnp.sqrt(energy_sum.reshape(-1) / pixel_count + 1e-06)
    inv_blocks = inverse.reshape(local_blocks + 2 * REACH, block)

    inv_left = lax.dynamic_slice_in_dim(
        jnp.take(inv_blocks, relative[:, 0], axis=0), offset, rows, 1
    )
    inv_right = jnp.take(inv_blocks, relative[:, 1], axis=0)
    rules = jnp.take(rule_of_block, pairs[:, 1], axis=0)
    source = (rules // per_index - me_ion) % ions
    slot = (source % 2) * 8 + ((source // 2) % 4) * 2 + source // 8
    rules = slot * per_index + rules % per_index
    matrices = jnp.take(lookup_tables, rules, axis=0)
    coloc = (gram * inv_left[:, :, None] * inv_right[:, None, :] / pixel_count).astype(jnp.bfloat16)
    scores = jnp.einsum("src,scd->srd", coloc, matrices, preferred_element_type=jnp.float32)
    used = jnp.arange(slots, dtype=jnp.int32) < live[0]
    scores = jnp.where(used[:, None, None], scores, 0.0).astype(jnp.bfloat16)
    return (smoothed, scores)


def solution(mesh):
    return jax.shard_map(
        on_device,
        mesh=mesh,
        in_specs=(
            P("ion", "pix"),
            P(None, "pix"),
            P("ion", None),
            P("ion"),
            P(),
            P("ion", None, None),
        ),
        out_specs=(P("ion", "pix"), P("ion", "pix", None)),
        check_vma=False,
    )
```

```python
import jax
import jax.numpy as jnp
from jax import lax
from jax.experimental import pallas as pl
from jax.experimental.pallas import tpu as pltpu
from jax.sharding import PartitionSpec as P

REACH = 3


def extended_2(array, sides, width):
    for axis, dim in sides:
        size, length = (lax.axis_size(axis), array.shape[dim])
        up = [(i, (i + 1) % size) for i in range(size - 1)]
        down = [(j, i) for i, j in up]
        last = lax.slice_in_dim(array, length - width, length, axis=dim)
        first = lax.slice_in_dim(array, 0, width, axis=dim)
        before = lax.ppermute(last, axis, up)
        after = lax.ppermute(first, axis, down)
        array = jnp.concatenate([before, array, after], axis=dim)
    return array


def gram_kernel(shares, rel_ref, before_ref, local_ref, after_ref, chunk_ref, out_ref, table_out,
                ext_ref, table, sems, send_sems, recv_sems):
    block = out_ref.shape[-1]
    slots = out_ref.shape[-3]
    rows = out_ref.shape[-2]
    width = before_ref.shape[0]
    middle = local_ref.shape[0]
    p = lax.axis_index("pix")
    c = p % 2
    x = (p // 2) % 4
    yl = p // 8
    partner = p + 1 - 2 * c
    right = (yl * 4 + (x + 1) % 4) * 2 + c
    left = (yl * 4 + (x + 3) % 4) * 2 + c
    ypart = ((1 - yl) * 4 + x) * 2 + c
    mine = c * 8 + x * 2 + yl
    theirs = c * 8 + x * 2 + 1 - yl
    pair_at = c * 8 + x * 2
    from_left = c * 8 + ((x + 3) % 4) * 2

    barrier = pltpu.get_barrier_semaphore()
    for peer in (partner, right, left, ypart):
        pl.semaphore_signal(barrier, 1, device_id={"pix": peer}, device_id_type=MESH)
    pl.semaphore_wait(barrier, 4)

    def remote(src, dst, k, peer):
        return pltpu.make_async_remote_copy(
            src_ref=src, dst_ref=dst, send_sem=send_sems.at[k], recv_sem=recv_sems.at[k],
            device_id={"pix": peer}, device_id_type=MESH,
        )

    sent = []
    ca = remote(chunk_ref, table.at[mine], 0, ypart)
    ca.start()
    sent.append(ca)
    own = pltpu.make_async_copy(chunk_ref, table.at[mine], sems.at[3])
    own.start()

    copies = [
        pltpu.make_async_copy(local_ref, ext_ref.at[pl.ds(width, middle)], sems.at[0]),
        pltpu.make_async_copy(before_ref, ext_ref.at[pl.ds(0, width)], sems.at[1]),
        pltpu.make_async_copy(after_ref, ext_ref.at[pl.ds(width + middle, width)], sems.at[2]),
    ]
    for cp in copies:
        cp.start()
    for cp in copies:
        cp.wait()

    def body(t, carry):
        left_rows = jnp.concatenate([ext_ref[rel_ref[4 * t]], ext_ref[rel_ref[4 * t + 2]]], axis=0)
        right_rows = jnp.concatenate([ext_ref[rel_ref[4 * t + 1]], ext_ref[rel_ref[4 * t + 3]]], axis=0)
        g = lax.dot_general(
            left_rows, right_rows, (((1,), (1,)), ((), ())), preferred_element_type=jnp.float32
        )
        for half in range(2):
            part = g[half * block : (half + 1) * block, half * block : (half + 1) * block]
            for q in range(shares):
                out_ref[q % 2, (q // 2) % 4, q // 8, 2 * t + half] = part[q * rows : (q + 1) * rows, :]
        return carry

    third = slots // 8
    lax.fori_loop(0, third, body, 0)
    ca.wait_recv()
    b1 = [
        remote(chunk_ref, table.at[mine], 1, right),
        remote(table.at[theirs], table.at[theirs], 2, right),
        remote(chunk_ref, table.at[mine], 3, left),
        remote(table.at[theirs], table.at[theirs], 4, left),
    ]
    for cp in b1:
        cp.start()
    sent += b1
    lax.fori_loop(third, 2 * third, body, 0)
    for cp in b1:
        cp.wait_recv()
    b2 = remote(table.at[pl.ds(from_left, 2)], table.at[pl.ds(from_left, 2)], 5, right)
    b2.start()
    sent.append(b2)
    lax.fori_loop(2 * third, 3 * third, body, 0)
    b2.wait_recv()
    own.wait()
    cc = remote(table.at[pl.ds(c * 8, 8)], table.at[pl.ds(c * 8, 8)], 6, partner)
    cc.start()
    sent.append(cc)
    lax.fori_loop(3 * third, slots // 2, body, 0)
    cc.wait_recv()
    for cp in sent:
        cp.wait_send()
    table_out[...] = table[...]


def pair_grams(relative, before, local, after, chunk, shares, block):
    slots = relative.shape[0]
    rows = block // shares
    pix_local = local.shape[1]
    ext_blocks = (before.shape[0] + local.shape[0] + after.shape[0]) // block
    ext_rows = ext_blocks * block
    flat = relative.reshape(-1).astype(jnp.int32)
    table_shape = (shares,) + chunk.shape
    before, local, after = (a.reshape(-1, block, pix_local) for a in (before, local, after))
    return pl.pallas_call(
        lambda *refs: gram_kernel(shares, *refs),
        out_shape=(
            jax.ShapeDtypeStruct((2, 4, 2, slots, rows, block), jnp.float32),
            jax.ShapeDtypeStruct(table_shape, chunk.dtype),
        ),
        in_specs=[pl.BlockSpec(memory_space=pltpu.SMEM)]
        + [pl.BlockSpec(memory_space=pl.ANY)] * 3
        + [pl.BlockSpec(memory_space=pltpu.VMEM)],
        out_specs=(pl.BlockSpec(memory_space=pltpu.VMEM),) * 2,
        scratch_shapes=[
            pltpu.VMEM((ext_blocks, block, pix_local), local.dtype),
            pltpu.VMEM(table_shape, chunk.dtype),
            pltpu.SemaphoreType.DMA((4,)),
            pltpu.SemaphoreType.DMA((7,)),
            pltpu.SemaphoreType.DMA((7,)),
        ],
        compiler_params=pltpu.CompilerParams(
            collective_id=1, has_side_effects=True, vmem_limit_bytes=56 * 1024 * 1024
        ),
        cost_estimate=pl.CostEstimate(
            flops=2 * slots * block * block * pix_local,
            transcendentals=0,
            bytes_accessed=ext_rows * pix_local * 2 + slots * block * block * 4,
        ),
    )(flat, before, local, after, chunk)

MESH = pl.DeviceIdType.MESH


def scatter_kernel(g_ref, e_ref, out_ref, eout_ref, r1, s1, recv_r, recv_l, acc_r, acc_l, tbuf, r3, ebuf, send_sem, recv_sem):
    p = lax.axis_index("pix")
    c = p % 2
    x = (p // 2) % 4
    yl = p // 8
    partner = p + 1 - 2 * c
    right = (yl * 4 + (x + 1) % 4) * 2 + c
    left = (yl * 4 + (x + 3) % 4) * 2 + c
    ypart = ((1 - yl) * 4 + x) * 2 + c

    barrier = pltpu.get_barrier_semaphore()
    for peer in (partner, right, left, ypart):
        pl.semaphore_signal(barrier, 1, device_id={"pix": peer}, device_id_type=MESH)
    pl.semaphore_wait(barrier, 4)

    def remote(src, dst, k, peer):
        return pltpu.make_async_remote_copy(
            src_ref=src, dst_ref=dst, send_sem=send_sem.at[k], recv_sem=recv_sem.at[k],
            device_id={"pix": peer}, device_id_type=MESH,
        )

    order = [(x + 3) % 4, (x + 1) % 4, (x + 2) % 4, x]
    stage1 = []
    for n, j in enumerate(order):
        cp = remote(g_ref.at[1 - c, j], r1.at[j], 12 + n if n else 0, partner)
        cp.start()
        stage1.append(cp)
    ce1 = remote(e_ref, ebuf.at[0], 1, partner)
    ce1.start()

    def settle(n):
        stage1[n].wait()
        s1[order[n]] = g_ref[c, order[n]] + r1[order[n]]

    settle(0)
    settle(1)
    ce1.wait()
    ebuf[1] = e_ref[...] + ebuf[0]

    done = []
    cr = cl = None
    for k in range(3):
        jr = (x + 3 - k) % 4
        jl = (x + k + 1) % 4
        if k == 0:
            src_r, src_l = s1.at[jr, 0], s1.at[jl, 1]
        else:
            if k == 1:
                settle(2)
            cr.wait_recv()
            cl.wait_recv()
            acc_r[k] = s1[jr, 0] + recv_r[k - 1]
            acc_l[k] = s1[jl, 1] + recv_l[k - 1]
            src_r, src_l = acc_r.at[k], acc_l.at[k]
        cr = remote(src_r, recv_r.at[k], 2 + k, right)
        cr.start()
        cl = remote(src_l, recv_l.at[k], 5 + k, left)
        cl.start()
        done += [cr, cl]
        if k == 0:
            er = remote(ebuf.at[1], ebuf.at[2], 8, right)
            er.start()
            el = remote(ebuf.at[1], ebuf.at[3], 9, left)
            el.start()
            done += [er, el]
        if k == 1:
            er.wait_recv()
            ef = remote(ebuf.at[2], ebuf.at[4], 10, right)
            ef.start()
            done.append(ef)
    settle(3)
    cr.wait_recv()
    cl.wait_recv()
    tbuf[0] = s1[x, 0] + recv_r[2]
    tbuf[1] = s1[x, 1] + recv_l[2]
    el.wait_recv()
    ef.wait_recv()
    ebuf[5] = ebuf[1] + ebuf[2] + ebuf[3] + ebuf[4]

    c3 = remote(tbuf.at[1 - yl], r3, 11, ypart)
    c3.start()
    ce3 = remote(ebuf.at[5], ebuf.at[6], 12, ypart)
    ce3.start()
    c3.wait()
    ce3.wait()
    out_ref[...] = tbuf[yl] + r3[...]
    eout_ref[...] = ebuf[5] + ebuf[6]
    for d in done:
        d.wait_send()


def scatter_grams(grams, energy_part):
    slots, rows, block = grams.shape[-3:]
    part = (slots, rows, block)
    f32 = jnp.float32
    return pl.pallas_call(
        scatter_kernel,
        out_shape=(
            jax.ShapeDtypeStruct(part, f32),
            jax.ShapeDtypeStruct(energy_part.shape, f32),
        ),
        in_specs=[pl.BlockSpec(memory_space=pltpu.VMEM)] * 2,
        out_specs=(pl.BlockSpec(memory_space=pltpu.VMEM),) * 2,
        scratch_shapes=[
            pltpu.VMEM((4, 2) + part, f32),
            pltpu.VMEM((4, 2) + part, f32),
            pltpu.VMEM((3,) + part, f32),
            pltpu.VMEM((3,) + part, f32),
            pltpu.VMEM((3,) + part, f32),
            pltpu.VMEM((3,) + part, f32),
            pltpu.VMEM((2,) + part, f32),
            pltpu.VMEM(part, f32),
            pltpu.VMEM((7,) + energy_part.shape, f32),
            pltpu.SemaphoreType.DMA((16,)),
            pltpu.SemaphoreType.DMA((16,)),
        ],
        compiler_params=pltpu.CompilerParams(
            collective_id=0, has_side_effects=True, vmem_limit_bytes=48 * 1024 * 1024
        ),
    )(grams, energy_part)


def smooth_rows(padded, stencil):
    pix_local = stencil.shape[1]
    total = jnp.zeros((padded.shape[0], pix_local), jnp.float32)
    for tap in range(5):
        total = total + stencil[tap][None, :] * padded[:, tap : tap + pix_local].astype(jnp.float32)
    return total.astype(jnp.bfloat16)


def row_squares(rows):
    values = rows.astype(jnp.float32)
    return jnp.sum(values * values, axis=1)


def on_device(images, stencil, pairs, live, rule_of_block, adduct):
    local_rows, pix_local = images.shape
    block = adduct.shape[1]
    local_blocks = local_rows // block
    shares = lax.axis_size("pix")
    rows = block // shares
    width = REACH * block
    ions = lax.axis_size("ion")
    up = [(i, i + 1) for i in range(ions - 1)]
    down = [(j, i) for i, j in up]
    raw_before = lax.ppermute(images[local_rows - width :], "ion", up)
    raw_after = lax.ppermute(images[:width], "ion", down)
    me_pix = lax.axis_index("pix")
    offset = me_pix * rows
    me_pix = lax.axis_index("pix")
    me_ion = lax.axis_index("ion")
    per_index = adduct.shape[0]
    turn = [
        (p * ions + j, p * ions + (j - p) % ions)
        for j in range(ions)
        for p in range(1, shares)
    ]
    fetched = lax.ppermute(adduct, ("pix", "ion"), turn)
    own_turn = jnp.where(me_pix == 0, adduct, fetched)
    padded = extended_2(images, (("pix", 1),), 2)
    smoothed = smooth_rows(padded, stencil)
    local_squares = row_squares(smoothed)
    edges = jnp.concatenate([padded[:, :2], padded[:, pix_local + 2 :]], axis=1)
    edge_before = lax.ppermute(edges[local_rows - width :], "ion", up)
    edge_after = lax.ppermute(edges[:width], "ion", down)
    before = smooth_rows(
        jnp.concatenate([edge_before[:, :2], raw_before, edge_before[:, 2:]], axis=1), stencil
    )
    after = smooth_rows(
        jnp.concatenate([edge_after[:, :2], raw_after, edge_after[:, 2:]], axis=1), stencil
    )
    squares = jnp.concatenate([row_squares(before), local_squares, row_squares(after)])
    pixel_count = pix_local * shares
    first = lax.axis_index("ion") * local_blocks
    slots = pairs.shape[0]
    relative = pairs - first + REACH

    grams, lookup_tables = pair_grams(relative, before, smoothed, after, own_turn, shares, block)
    lookup_tables = lookup_tables.reshape((-1,) + adduct.shape[1:])
    gram, energy_sum = scatter_grams(grams, squares.reshape(-1, block))
    inverse = 1.0 / jnp.sqrt(energy_sum.reshape(-1) / pixel_count + 1e-06)
    inv_blocks = inverse.reshape(local_blocks + 2 * REACH, block)

    inv_left = lax.dynamic_slice_in_dim(
        jnp.take(inv_blocks, relative[:, 0], axis=0), offset, rows, 1
    )
    inv_right = jnp.take(inv_blocks, relative[:, 1], axis=0)
    rules = jnp.take(rule_of_block, pairs[:, 1], axis=0)
    source = (rules // per_index - me_ion) % ions
    slot = (source % 2) * 8 + ((source // 2) % 4) * 2 + source // 8
    rules = slot * per_index + rules % per_index
    matrices = jnp.take(lookup_tables, rules, axis=0)
    coloc = (gram * inv_left[:, :, None] * inv_right[:, None, :] / pixel_count).astype(jnp.bfloat16)
    scores = jnp.einsum("src,scd->srd", coloc, matrices, preferred_element_type=jnp.float32)
    used = jnp.arange(slots, dtype=jnp.int32) < live[0]
    scores = jnp.where(used[:, None, None], scores, 0.0).astype(jnp.bfloat16)
    return (smoothed, scores)


def solution(mesh):
    return jax.shard_map(
        on_device,
        mesh=mesh,
        in_specs=(
            P("ion", "pix"),
            P(None, "pix"),
            P("ion", None),
            P("ion"),
            P(),
            P("ion", None, None),
        ),
        out_specs=(P("ion", "pix"), P("ion", "pix", None)),
        check_vma=False,
    )
```

```python
import jax
import jax.numpy as jnp
from jax import lax
from jax.experimental import pallas as pl
from jax.experimental.pallas import tpu as pltpu
from jax.sharding import PartitionSpec as P

REACH = 3


def extended_2(array, sides, width):
    for axis, dim in sides:
        size, length = (lax.axis_size(axis), array.shape[dim])
        up = [(i, (i + 1) % size) for i in range(size - 1)]
        down = [(j, i) for i, j in up]
        last = lax.slice_in_dim(array, length - width, length, axis=dim)
        first = lax.slice_in_dim(array, 0, width, axis=dim)
        before = lax.ppermute(last, axis, up)
        after = lax.ppermute(first, axis, down)
        array = jnp.concatenate([before, array, after], axis=dim)
    return array


def gram_kernel(shares, rel_ref, before_ref, local_ref, after_ref, chunk_ref, out_ref, table_out,
                ext_ref, table, sems, send_sems, recv_sems):
    block = out_ref.shape[-1]
    slots = out_ref.shape[-3]
    rows = out_ref.shape[-2]
    width = before_ref.shape[0]
    middle = local_ref.shape[0]
    p = lax.axis_index("pix")
    c = p % 2
    x = (p // 2) % 4
    yl = p // 8
    partner = p + 1 - 2 * c
    right = (yl * 4 + (x + 1) % 4) * 2 + c
    left = (yl * 4 + (x + 3) % 4) * 2 + c
    ypart = ((1 - yl) * 4 + x) * 2 + c
    mine = c * 8 + x * 2 + yl
    theirs = c * 8 + x * 2 + 1 - yl
    pair_at = c * 8 + x * 2
    from_left = c * 8 + ((x + 3) % 4) * 2

    barrier = pltpu.get_barrier_semaphore()
    for peer in (partner, right, left, ypart):
        pl.semaphore_signal(barrier, 1, device_id={"pix": peer}, device_id_type=MESH)
    pl.semaphore_wait(barrier, 4)

    def remote(src, dst, k, peer):
        return pltpu.make_async_remote_copy(
            src_ref=src, dst_ref=dst, send_sem=send_sems.at[k], recv_sem=recv_sems.at[k],
            device_id={"pix": peer}, device_id_type=MESH,
        )

    sent = []
    ca = remote(chunk_ref, table.at[mine], 0, ypart)
    ca.start()
    sent.append(ca)
    own = pltpu.make_async_copy(chunk_ref, table.at[mine], sems.at[3])
    own.start()

    copies = [
        pltpu.make_async_copy(local_ref, ext_ref.at[pl.ds(width, middle)], sems.at[0]),
        pltpu.make_async_copy(before_ref, ext_ref.at[pl.ds(0, width)], sems.at[1]),
        pltpu.make_async_copy(after_ref, ext_ref.at[pl.ds(width + middle, width)], sems.at[2]),
    ]
    for cp in copies:
        cp.start()
    for cp in copies:
        cp.wait()

    def body(t, carry):
        left_rows = jnp.concatenate([ext_ref[rel_ref[4 * t]], ext_ref[rel_ref[4 * t + 2]]], axis=0)
        right_rows = jnp.concatenate([ext_ref[rel_ref[4 * t + 1]], ext_ref[rel_ref[4 * t + 3]]], axis=0)
        g = lax.dot_general(
            left_rows, right_rows, (((1,), (1,)), ((), ())), preferred_element_type=jnp.float32
        )
        for half in range(2):
            part = g[half * block : (half + 1) * block, half * block : (half + 1) * block]
            for q in range(shares):
                out_ref[q % 2, (q // 2) % 4, q // 8, 2 * t + half] = part[q * rows : (q + 1) * rows, :]
        return carry

    third = slots // 8
    lax.fori_loop(0, third, body, 0)
    ca.wait_recv()
    b1 = [
        remote(chunk_ref, table.at[mine], 1, right),
        remote(table.at[theirs], table.at[theirs], 2, right),
        remote(chunk_ref, table.at[mine], 3, left),
        remote(table.at[theirs], table.at[theirs], 4, left),
    ]
    for cp in b1:
        cp.start()
    sent += b1
    lax.fori_loop(third, 2 * third, body, 0)
    for cp in b1:
        cp.wait_recv()
    b2 = remote(table.at[pl.ds(from_left, 2)], table.at[pl.ds(from_left, 2)], 5, right)
    b2.start()
    sent.append(b2)
    lax.fori_loop(2 * third, 3 * third, body, 0)
    b2.wait_recv()
    own.wait()
    cc = remote(table.at[pl.ds(c * 8, 8)], table.at[pl.ds(c * 8, 8)], 6, partner)
    cc.start()
    sent.append(cc)
    lax.fori_loop(3 * third, slots // 2, body, 0)
    cc.wait_recv()
    for cp in sent:
        cp.wait_send()
    table_out[...] = table[...]


def pair_grams(relative, before, local, after, chunk, shares, block):
    slots = relative.shape[0]
    rows = block // shares
    pix_local = local.shape[1]
    ext_blocks = (before.shape[0] + local.shape[0] + after.shape[0]) // block
    ext_rows = ext_blocks * block
    flat = relative.reshape(-1).astype(jnp.int32)
    table_shape = (shares,) + chunk.shape
    before, local, after = (a.reshape(-1, block, pix_local) for a in (before, local, after))
    return pl.pallas_call(
        lambda *refs: gram_kernel(shares, *refs),
        out_shape=(
            jax.ShapeDtypeStruct((2, 4, 2, slots, rows, block), jnp.float32),
            jax.ShapeDtypeStruct(table_shape, chunk.dtype),
        ),
        in_specs=[pl.BlockSpec(memory_space=pltpu.SMEM)]
        + [pl.BlockSpec(memory_space=pl.ANY)] * 3
        + [pl.BlockSpec(memory_space=pltpu.VMEM)],
        out_specs=(pl.BlockSpec(memory_space=pltpu.VMEM),) * 2,
        scratch_shapes=[
            pltpu.VMEM((ext_blocks, block, pix_local), local.dtype),
            pltpu.VMEM(table_shape, chunk.dtype),
            pltpu.SemaphoreType.DMA((4,)),
            pltpu.SemaphoreType.DMA((7,)),
            pltpu.SemaphoreType.DMA((7,)),
        ],
        compiler_params=pltpu.CompilerParams(
            collective_id=1, has_side_effects=True, vmem_limit_bytes=56 * 1024 * 1024
        ),
        cost_estimate=pl.CostEstimate(
            flops=2 * slots * block * block * pix_local,
            transcendentals=0,
            bytes_accessed=ext_rows * pix_local * 2 + slots * block * block * 4,
        ),
    )(flat, before, local, after, chunk)

MESH = pl.DeviceIdType.MESH


def scatter_kernel(g_ref, e_ref, out_ref, eout_ref, r1, s1, recv_r, recv_l, acc_r, acc_l, tbuf, r3, ebuf, send_sem, recv_sem):
    p = lax.axis_index("pix")
    c = p % 2
    x = (p // 2) % 4
    yl = p // 8
    partner = p + 1 - 2 * c
    right = (yl * 4 + (x + 1) % 4) * 2 + c
    left = (yl * 4 + (x + 3) % 4) * 2 + c
    ypart = ((1 - yl) * 4 + x) * 2 + c

    barrier = pltpu.get_barrier_semaphore()
    for peer in (partner, right, left, ypart):
        pl.semaphore_signal(barrier, 1, device_id={"pix": peer}, device_id_type=MESH)
    pl.semaphore_wait(barrier, 4)

    def remote(src, dst, k, peer):
        return pltpu.make_async_remote_copy(
            src_ref=src, dst_ref=dst, send_sem=send_sem.at[k], recv_sem=recv_sem.at[k],
            device_id={"pix": peer}, device_id_type=MESH,
        )

    order = [
        ((x + 3) % 4, 0), ((x + 1) % 4, 1), ((x + 2) % 4, 0), ((x + 2) % 4, 1),
        ((x + 1) % 4, 0), ((x + 3) % 4, 1), (x, 0), (x, 1),
    ]
    stage1 = []
    for n, (j, h) in enumerate(order):
        cp = remote(g_ref.at[1 - c, j, h], r1.at[j, h], 12 + n if n else 0, partner)
        cp.start()
        stage1.append(cp)
    ce1 = remote(e_ref, ebuf.at[0], 1, partner)
    ce1.start()

    def settle(n):
        j, h = order[n]
        stage1[n].wait()
        s1[j, h] = g_ref[c, j, h] + r1[j, h]

    settle(0)
    settle(1)
    ce1.wait()
    ebuf[1] = e_ref[...] + ebuf[0]

    done = []
    cr = cl = None
    for k in range(3):
        jr = (x + 3 - k) % 4
        jl = (x + k + 1) % 4
        if k == 0:
            src_r, src_l = s1.at[jr, 0], s1.at[jl, 1]
        else:
            settle(2 * k)
            settle(2 * k + 1)
            cr.wait_recv()
            cl.wait_recv()
            acc_r[k] = s1[jr, 0] + recv_r[k - 1]
            acc_l[k] = s1[jl, 1] + recv_l[k - 1]
            src_r, src_l = acc_r.at[k], acc_l.at[k]
        cr = remote(src_r, recv_r.at[k], 2 + k, right)
        cr.start()
        cl = remote(src_l, recv_l.at[k], 5 + k, left)
        cl.start()
        done += [cr, cl]
        if k == 0:
            er = remote(ebuf.at[1], ebuf.at[2], 8, right)
            er.start()
            el = remote(ebuf.at[1], ebuf.at[3], 9, left)
            el.start()
            done += [er, el]
        if k == 1:
            er.wait_recv()
            ef = remote(ebuf.at[2], ebuf.at[4], 10, right)
            ef.start()
            done.append(ef)
    settle(6)
    settle(7)
    cr.wait_recv()
    cl.wait_recv()
    tbuf[0] = s1[x, 0] + recv_r[2]
    tbuf[1] = s1[x, 1] + recv_l[2]
    el.wait_recv()
    ef.wait_recv()
    ebuf[5] = ebuf[1] + ebuf[2] + ebuf[3] + ebuf[4]

    c3 = remote(tbuf.at[1 - yl], r3, 11, ypart)
    c3.start()
    ce3 = remote(ebuf.at[5], ebuf.at[6], 12, ypart)
    ce3.start()
    c3.wait()
    ce3.wait()
    out_ref[...] = tbuf[yl] + r3[...]
    eout_ref[...] = ebuf[5] + ebuf[6]
    for d in done:
        d.wait_send()


def scatter_grams(grams, energy_part):
    slots, rows, block = grams.shape[-3:]
    part = (slots, rows, block)
    f32 = jnp.float32
    return pl.pallas_call(
        scatter_kernel,
        out_shape=(
            jax.ShapeDtypeStruct(part, f32),
            jax.ShapeDtypeStruct(energy_part.shape, f32),
        ),
        in_specs=[pl.BlockSpec(memory_space=pltpu.VMEM)] * 2,
        out_specs=(pl.BlockSpec(memory_space=pltpu.VMEM),) * 2,
        scratch_shapes=[
            pltpu.VMEM((4, 2) + part, f32),
            pltpu.VMEM((4, 2) + part, f32),
            pltpu.VMEM((3,) + part, f32),
            pltpu.VMEM((3,) + part, f32),
            pltpu.VMEM((3,) + part, f32),
            pltpu.VMEM((3,) + part, f32),
            pltpu.VMEM((2,) + part, f32),
            pltpu.VMEM(part, f32),
            pltpu.VMEM((7,) + energy_part.shape, f32),
            pltpu.SemaphoreType.DMA((20,)),
            pltpu.SemaphoreType.DMA((20,)),
        ],
        compiler_params=pltpu.CompilerParams(
            collective_id=0, has_side_effects=True, vmem_limit_bytes=48 * 1024 * 1024
        ),
    )(grams, energy_part)


def smooth_rows(padded, stencil):
    pix_local = stencil.shape[1]
    total = jnp.zeros((padded.shape[0], pix_local), jnp.float32)
    for tap in range(5):
        total = total + stencil[tap][None, :] * padded[:, tap : tap + pix_local].astype(jnp.float32)
    return total.astype(jnp.bfloat16)


def row_squares(rows):
    values = rows.astype(jnp.float32)
    return jnp.sum(values * values, axis=1)


def on_device(images, stencil, pairs, live, rule_of_block, adduct):
    local_rows, pix_local = images.shape
    block = adduct.shape[1]
    local_blocks = local_rows // block
    shares = lax.axis_size("pix")
    rows = block // shares
    width = REACH * block
    ions = lax.axis_size("ion")
    up = [(i, i + 1) for i in range(ions - 1)]
    down = [(j, i) for i, j in up]
    raw_before = lax.ppermute(images[local_rows - width :], "ion", up)
    raw_after = lax.ppermute(images[:width], "ion", down)
    me_pix = lax.axis_index("pix")
    offset = me_pix * rows
    me_pix = lax.axis_index("pix")
    me_ion = lax.axis_index("ion")
    per_index = adduct.shape[0]
    turn = [
        (p * ions + j, p * ions + (j - p) % ions)
        for j in range(ions)
        for p in range(1, shares)
    ]
    fetched = lax.ppermute(adduct, ("pix", "ion"), turn)
    own_turn = jnp.where(me_pix == 0, adduct, fetched)
    padded = extended_2(images, (("pix", 1),), 2)
    smoothed = smooth_rows(padded, stencil)
    local_squares = row_squares(smoothed)
    edges = jnp.concatenate([padded[:, :2], padded[:, pix_local + 2 :]], axis=1)
    edge_before = lax.ppermute(edges[local_rows - width :], "ion", up)
    edge_after = lax.ppermute(edges[:width], "ion", down)
    before = smooth_rows(
        jnp.concatenate([edge_before[:, :2], raw_before, edge_before[:, 2:]], axis=1), stencil
    )
    after = smooth_rows(
        jnp.concatenate([edge_after[:, :2], raw_after, edge_after[:, 2:]], axis=1), stencil
    )
    squares = jnp.concatenate([row_squares(before), local_squares, row_squares(after)])
    pixel_count = pix_local * shares
    first = lax.axis_index("ion") * local_blocks
    slots = pairs.shape[0]
    relative = pairs - first + REACH

    grams, lookup_tables = pair_grams(relative, before, smoothed, after, own_turn, shares, block)
    lookup_tables = lookup_tables.reshape((-1,) + adduct.shape[1:])
    gram, energy_sum = scatter_grams(grams, squares.reshape(-1, block))
    inverse = 1.0 / jnp.sqrt(energy_sum.reshape(-1) / pixel_count + 1e-06)
    inv_blocks = inverse.reshape(local_blocks + 2 * REACH, block)

    inv_left = lax.dynamic_slice_in_dim(
        jnp.take(inv_blocks, relative[:, 0], axis=0), offset, rows, 1
    )
    inv_right = jnp.take(inv_blocks, relative[:, 1], axis=0)
    rules = jnp.take(rule_of_block, pairs[:, 1], axis=0)
    source = (rules // per_index - me_ion) % ions
    slot = (source % 2) * 8 + ((source // 2) % 4) * 2 + source // 8
    rules = slot * per_index + rules % per_index
    matrices = jnp.take(lookup_tables, rules, axis=0)
    coloc = (gram * inv_left[:, :, None] * inv_right[:, None, :] / pixel_count).astype(jnp.bfloat16)
    scores = jnp.einsum("src,scd->srd", coloc, matrices, preferred_element_type=jnp.float32)
    used = jnp.arange(slots, dtype=jnp.int32) < live[0]
    scores = jnp.where(used[:, None, None], scores, 0.0).astype(jnp.bfloat16)
    return (smoothed, scores)


def solution(mesh):
    return jax.shard_map(
        on_device,
        mesh=mesh,
        in_specs=(
            P("ion", "pix"),
            P(None, "pix"),
            P("ion", None),
            P("ion"),
            P(),
            P("ion", None, None),
        ),
        out_specs=(P("ion", "pix"), P("ion", "pix", None)),
        check_vma=False,
    )
```
